32 devices in a mesh: groups: 2 (over y), seq: 4 (over z), head: 4 (over x, core).
Axes of the slice: x: 2, y: 2, z: 4, core: 2. Of those that a mesh axis runs over, the one named last changes fastest.
Arguments:
- q_feat: bfloat16 [8192, 256], P(('groups', 'seq'), 'head'), parts along dimension 0, may hold values from -4 to 4
- k_feat: bfloat16 [8192, 256], P(('groups', 'seq'), 'head'), parts along dimension 0, may hold values from -4 to 4
- swa_query: bfloat16 [8192, 2048], P(('groups', 'seq'), 'head'), parts along dimension 0, may hold values from -4.25 to 4.25
- swa_key: bfloat16 [8192, 2048], P(('groups', 'seq'), 'head'), parts along dimension 0, may hold values from -4.25 to 4.25
- values: bfloat16 [8192, 2048], P(('groups', 'seq'), 'head'), parts along dimension 0, may hold values from -6 to 6
- gain: float32 [2048], P('head'), may hold values from 0.5 to 1.5
Outputs:
- mixed_out: bfloat16 [8192, 2048], P(('groups', 'seq'), 'head'), parts along dimension 0
The draws below stay inside these ranges and needn't reach their ends.
There are 2 independent parts, one for each index of `groups`. The reference program is written for one: setup_inputs(seed, part) draws one part's arguments, and reference() takes and returns one part's arrays. A program takes and returns all parts, laid end to end along the dimension named above; an argument that names none is the same for every part. Nothing has to cross between parts.
All inputs are finite; a program needn't handle non-finite values.
Results may differ from the reference program's by a relative error of at most 0.0044.
Values may be sent and summed in bfloat16 or wider, within the bound.
No kernel may reach another device: no remote copies, remote signals or barrier semaphores. Data moves between devices by JAX's collectives and lax.ppermute only.
A program may use at most 128 MiB of HBM per device.

```python
import jax
import jax.numpy as jnp
from jax import lax

HEADS = 16
HEAD_DIM = 128
FEAT = 16
WINDOW = 512
NFEAT = 273
SEQ_LEN = 4096


def draw_pair(key):
    base_key = jax.random.fold_in(key, 4242)
    key_query, key_keys = jax.random.split(base_key, 2)
    width = HEADS * HEAD_DIM
    query = jnp.clip(jax.random.normal(key_query, (SEQ_LEN, width), jnp.float32), -4.0, 4.0)
    key_rows = jnp.clip(jax.random.normal(key_keys, (SEQ_LEN, width), jnp.float32), -4.0, 4.0)
    return (query, key_rows)


def draw_swa_query(key, part):
    return draw_pair(key)[0].astype(jnp.bfloat16)


def draw_swa_key(key, part):
    return draw_pair(key)[1].astype(jnp.bfloat16)


def block_levels(rng, dims, cuts, least, top_value):
    level = 1.0
    for position, shards_of in cuts:
        steps = jax.random.uniform(jax.random.fold_in(jax.random.fold_in(rng, 6), position), (shards_of,), jnp.float32, least / len(cuts), top_value / len(cuts))
        level = level * jnp.repeat(jnp.exp(steps), dims[position] // shards_of).reshape((-1,) + (1,) * (len(dims) - 1 - position))
    return level


def gaussian(stream_key, shape, deviation, most, cuts=(), kind=jnp.bfloat16):
    level = block_levels(stream_key, shape, cuts, -0.22, 0.18) if cuts else 1.0
    entries = jax.random.normal(stream_key, shape, jnp.float32) * deviation * level
    return jnp.minimum(jnp.maximum(entries, -most), most).astype(kind)


def setup_inputs(seed: int = 0, part: int = 0) -> dict:
    arg_keys = jax.random.split(jax.random.key(seed), 7)
    part_keys = jax.random.split(jax.random.fold_in(arg_keys[6], part), 7)
    q_feat = gaussian(part_keys[0], (SEQ_LEN, HEADS * FEAT), 1.0, 4.0, ((0, 4), (1, 4)))
    k_feat = gaussian(part_keys[1], (SEQ_LEN, HEADS * FEAT), 1.0, 4.0, ((0, 4), (1, 4)))
    swa_query = draw_swa_query(jax.random.fold_in(jax.random.fold_in(arg_keys[6], part), 71), part)
    swa_key = draw_swa_key(jax.random.fold_in(jax.random.fold_in(arg_keys[6], part), 71), part)
    values = gaussian(part_keys[4], (SEQ_LEN, HEADS * HEAD_DIM), 1.0, 6.0, ((0, 4), (1, 4)))
    gain = jnp.clip(1.0 + 0.1 * jax.random.normal(arg_keys[5], (HEADS * HEAD_DIM,), jnp.float32), 0.5, 1.5)
    return dict(q_feat=q_feat, k_feat=k_feat, swa_query=swa_query, swa_key=swa_key, values=values, gain=gain)


def features(vector):
    width = vector.shape[-1]
    outer_part = (vector[..., :, None] * vector[..., None, :]).reshape(vector.shape[:-1] + (width * width,))
    constant = jnp.ones(vector.shape[:-1] + (1,), jnp.float32)
    return jnp.concatenate([constant, vector * width ** (-0.25), outer_part * (0.5 ** 0.5 * width ** (-0.5))], -1)

def rounded(array):
    return lax.optimization_barrier(array.astype(jnp.bfloat16)).astype(jnp.float32)

def reference(q_feat, k_feat, swa_query, swa_key, values, gain):
    highest = lax.Precision.HIGHEST
    head_count = HEADS
    block_count = SEQ_LEN // WINDOW
    q_blocks = q_feat.reshape(block_count, WINDOW, head_count, FEAT)
    k_blocks = k_feat.reshape(block_count, WINDOW, head_count, FEAT)
    sq_blocks = swa_query.reshape(block_count, WINDOW, head_count * HEAD_DIM)
    sk_blocks = swa_key.reshape(block_count, WINDOW, head_count * HEAD_DIM)
    v_blocks = values.reshape(block_count, WINDOW, head_count * HEAD_DIM)
    block_ids = jnp.arange(block_count, dtype=jnp.int32)
    gain_rows = gain.reshape(head_count, HEAD_DIM)
    row_idx = jnp.arange(WINDOW)[:, None]
    col_wide = jnp.arange(2 * WINDOW)[None, :]
    col_near = jnp.arange(WINDOW)[None, :]

    def one_block(carry, inputs):
        state, norm_sum, prev_key, prev_value = carry
        qfb, kfb, sqb, skb, vb, block_idx = inputs
        first_pos = block_idx * WINDOW
        query3 = sqb.astype(jnp.float32).reshape(WINDOW, head_count, HEAD_DIM)
        key_rows = jnp.concatenate([prev_key, skb], 0).astype(jnp.float32).reshape(2 * WINDOW, head_count, HEAD_DIM)
        val_rows = jnp.concatenate([prev_value, vb], 0).astype(jnp.float32).reshape(2 * WINDOW, head_count, HEAD_DIM)
        scores = jnp.einsum('ihe,jhe->hij', query3, key_rows, precision=highest) * HEAD_DIM ** (-0.5)
        offset = WINDOW + row_idx - col_wide
        allowed = (offset >= 0) & (offset < WINDOW) & (first_pos - WINDOW + col_wide >= 0)
        scores = jnp.where(allowed[None], scores, -1e+30)
        top = lax.optimization_barrier(jnp.max(scores, -1, keepdims=True))
        expo = jnp.exp(scores - top)
        weights = rounded(expo / lax.optimization_barrier(jnp.sum(expo, -1, keepdims=True)))
        window_out = jnp.einsum('hij,jhe->ihe', weights, val_rows, precision=highest)
        qf32 = qfb.astype(jnp.float32)
        kf32 = kfb.astype(jnp.float32)
        vf32 = vb.astype(jnp.float32).reshape(WINDOW, head_count, HEAD_DIM)
        sim = jnp.einsum('ihf,jhf->hij', qf32, kf32, precision=highest) * FEAT ** (-0.5)
        taylor = rounded(jnp.where((col_near <= row_idx)[None], 1.0 + sim + 0.5 * sim * sim, 0.0))
        phi_query = rounded(features(qf32))
        phi_key = rounded(features(kf32))
        numer = jnp.einsum('hij,jhe->ihe', taylor, vf32, precision=highest)
        numer = numer + jnp.einsum('ihn,hne->ihe', phi_query, state, precision=highest)
        denom = lax.optimization_barrier(jnp.sum(taylor, -1)).T + jnp.einsum('ihn,hn->ih', phi_query, norm_sum, precision=highest)
        mixed = numer / denom[..., None] + window_out
        scale = lax.rsqrt(lax.optimization_barrier(jnp.mean(mixed * mixed, -1, keepdims=True)) + 1e-05)
        result = (mixed * scale * gain_rows[None]).reshape(WINDOW, head_count * HEAD_DIM).astype(jnp.bfloat16)
        state = state + jnp.einsum('jhn,jhe->hne', phi_key, vf32, precision=highest)
        norm_sum = norm_sum + lax.optimization_barrier(jnp.sum(phi_key, 0))
        return ((state, norm_sum, skb, vb), result)
    start = (jnp.zeros((head_count, NFEAT, HEAD_DIM), jnp.float32), jnp.zeros((head_count, NFEAT), jnp.float32), jnp.zeros((WINDOW, head_count * HEAD_DIM), jnp.bfloat16), jnp.zeros((WINDOW, head_count * HEAD_DIM), jnp.bfloat16))
    final_carry, outputs = lax.scan(one_block, start, (q_blocks, k_blocks, sq_blocks, sk_blocks, v_blocks, block_ids))
    return outputs.reshape(SEQ_LEN, head_count * HEAD_DIM)
```

```python
import functools

import jax
import jax.numpy as jnp
from jax import lax
from jax.experimental import pallas as pl
from jax.experimental.pallas import tpu as pltpu
from jax.sharding import PartitionSpec as P

HEAD_DIM = 128
WINDOW = 512
TILE = 256
NEG = -1e30
LOG2E = 1.4426950408889634
BF = jnp.bfloat16
F32 = jnp.float32


def feature_rows(width):
    return -(-(width * (width + 1) // 2 + width + 1) // 16) * 16


def state_rows(heads, width):
    return heads * feature_rows(width) + 16


def nt(a, b):
    return lax.dot_general(a, b, (((1,), (1,)), ((), ())), preferred_element_type=F32)


def nn(a, b):
    return jnp.dot(a, b, preferred_element_type=F32)


def phi_rows(x, query):
    width, tokens = x.shape
    half = width // 2
    scale = 0.5**0.5 * width ** (-0.5)
    twice = jnp.concatenate([x, x], 0)
    rows = []
    for d in range(half):
        prod = ((x * twice[d : d + width]) * scale).astype(BF)
        if query and d:
            prod = prod * 2
        rows.append(prod)
    rows.append((x * width ** (-0.25)).astype(BF))
    cross = (x[:half] * x[half:]) * scale
    if query:
        cross = cross * 2
    pad = feature_rows(width) - (half * width + width + half)
    last = lax.broadcasted_iota(jnp.int32, (pad, tokens), 0)
    const = jnp.where(last == 0, 1.0, 0.0)
    rows.append(jnp.concatenate([cross, const], 0).astype(BF))
    return jnp.concatenate(rows, 0)


def with_ones(v):
    return jnp.concatenate([v, jnp.ones_like(v)], 1)


def state_kernel(kf_ref, v_ref, first_ref, own_ref, *, heads, width, blocks):
    feats = feature_rows(width)
    base = heads * feats
    kft = kf_ref[...].astype(F32).T
    ones = jnp.ones((16, WINDOW), BF)
    first_ref[base:, :] = jnp.zeros((16, HEAD_DIM), F32)
    own_ref[base:, :] = jnp.zeros((16, HEAD_DIM), BF)
    for h in range(heads):
        phi = phi_rows(kft[h * width : (h + 1) * width], False)
        total, norm = None, None
        for b in range(blocks):
            part = phi[:, b * WINDOW : (b + 1) * WINDOW]
            s = nn(part, v_ref[b * WINDOW : (b + 1) * WINDOW, h * HEAD_DIM : (h + 1) * HEAD_DIM])
            n = nt(ones, part)
            total = s if b == 0 else total + s
            norm = n if b == 0 else norm + n
            if b == 0:
                first_ref[h * feats : (h + 1) * feats, :] = s
                first_ref[base + 2 * h : base + 2 * h + 1, :] = n[:1, :HEAD_DIM]
                first_ref[base + 2 * h + 1 : base + 2 * h + 2, : feats - HEAD_DIM] = n[:1, HEAD_DIM:]
        own_ref[h * feats : (h + 1) * feats, :] = total.astype(BF)
        own_ref[base + 2 * h : base + 2 * h + 1, :] = norm[:1, :HEAD_DIM].astype(BF)
        own_ref[base + 2 * h + 1 : base + 2 * h + 2, : feats - HEAD_DIM] = norm[:1, HEAD_DIM:].astype(BF)


def softmax_part(q, tiles):
    scale = HEAD_DIM ** (-0.5) * LOG2E
    scores = []
    for key, _, mask in tiles:
        s = nt(q, key)
        scores.append(s if mask is None else jnp.where(mask, s, NEG))
    top = functools.reduce(jnp.maximum, scores)
    top = jnp.max(top, 1, keepdims=True)
    acc = None
    for s, (_, value, _) in zip(scores, tiles):
        p = jnp.exp2((s - top) * scale).astype(BF)
        part = nn(p, with_ones(value))
        acc = part if acc is None else acc + part
    return top, acc[:, :HEAD_DIM], acc[:, HEAD_DIM:]


def local_kernel(q_ref, k_ref, v_ref, qf_ref, kf_ref, num_ref, den_ref, win_ref, sum_ref, top_ref, phi_ref, *, width, blocks):
    h = pl.program_id(0)
    row = lax.broadcasted_iota(jnp.int32, (TILE, TILE), 0)
    col = lax.broadcasted_iota(jnp.int32, (TILE, TILE), 1)
    causal = col <= row
    beyond = col > row
    lane = lax.broadcasted_iota(jnp.int32, (TILE, qf_ref.shape[1]), 1)
    mine = (lane >= h * width) & (lane < (h + 1) * width)
    tokens = q_ref.shape[0]
    for start in range(0, tokens, TILE):
        at = slice(start, start + TILE)
        q = q_ref[at, :]
        tiles = []
        for back, mask in ((WINDOW, beyond), (WINDOW - TILE, None), (0, causal)):
            key_at = start - back
            if key_at >= 0:
                ks = slice(key_at, key_at + TILE)
                tiles.append((k_ref[ks, :], v_ref[ks, :], mask))
        top, out, total = softmax_part(q, tiles)
        if start >= WINDOW:
            win_ref[at, :] = out / total
        else:
            win_ref[at, :] = out
            sum_ref[at, :] = total
            top_ref[at, :] = jnp.broadcast_to(top, (TILE, HEAD_DIM))
        qf = jnp.where(mine, qf_ref[at, :], jnp.zeros((), BF))
        acc = None
        for key_at in range(start - start % WINDOW, start + TILE, TILE):
            ks = slice(key_at, key_at + TILE)
            r = nt(qf, kf_ref[ks, :])
            t = (r * (0.5 / width) + width ** (-0.5)) * r + 1.0
            if key_at == start:
                t = jnp.where(causal, t, 0.0)
            part = nn(t.astype(BF), with_ones(v_ref[ks, :]))
            acc = part if acc is None else acc + part
        num_ref[at, :] = acc[:, :HEAD_DIM]
        den_ref[at, :] = acc[:, HEAD_DIM:]
    @pl.when(h == 0)
    def _():
        qft = qf_ref[...].astype(F32).T
        for g in range(qf_ref.shape[1] // width):
            phi_ref[g] = phi_rows(qft[g * width : (g + 1) * width], True).astype(F32).T.astype(BF)


def final_kernel(later_ref, q_ref, hk_ref, hv_ref, num_ref, den_ref, win_ref, sum_ref, top_ref, phi_ref, prior_ref, first_ref, gain_ref, out_ref, *, heads, width, blocks):
    h = pl.program_id(0)
    feats = feature_rows(width)
    base = heads * feats
    row = lax.broadcasted_iota(jnp.int32, (TILE, TILE), 0)
    col = lax.broadcasted_iota(jnp.int32, (TILE, TILE), 1)
    beyond = col > row
    scale = HEAD_DIM ** (-0.5) * LOG2E
    state = prior_ref[pl.ds(pl.multiple_of(h * feats, 16), feats), :]
    norm = [prior_ref[pl.ds(base + 2 * h + i, 1), :] for i in range(2)]
    add_state = first_ref[pl.ds(pl.multiple_of(h * feats, 16), feats), :]
    add_norm = [first_ref[pl.ds(base + 2 * h + i, 1), :] for i in range(2)]
    gain = gain_ref[...]

    def rhs(state, norm):
        wide = jnp.concatenate([jnp.broadcast_to(n, (HEAD_DIM, HEAD_DIM)) for n in norm], 1)
        cols = wide.T[:feats]
        return jnp.concatenate([state.astype(BF), cols.astype(BF)], 1)

    for b in range(blocks):
        if b == 1:
            state = state + add_state
            norm = [a + c for a, c in zip(norm, add_norm)]
        both = rhs(state, norm)
        for start in range(b * WINDOW, (b + 1) * WINDOW, TILE):
            at = slice(start, start + TILE)
            lin = nn(phi_ref[0, at, :], both)
            mixed = (num_ref[at, :] + lin[:, :HEAD_DIM]) / (den_ref[at, :] + lin[:, HEAD_DIM:])
            if b == 0:
                tiles = []
                for key_at in range(start, WINDOW, TILE):
                    ks = slice(key_at, key_at + TILE)
                    tiles.append((hk_ref[ks, :], hv_ref[ks, :], beyond if key_at == start else None))
                top, out, total = softmax_part(q_ref[at, :], tiles)
                top = jnp.where(later_ref[0] > 0, top, 2 * NEG)
                mine = top_ref[at, :]
                most = jnp.maximum(mine, top)
                here = jnp.exp2((mine - most) * scale)
                there = jnp.exp2((top - most) * scale)
                window = (win_ref[at, :] * here + out * there) / (sum_ref[at, :] * here + total * there)
            else:
                window = win_ref[at, :]
            mixed = mixed + window
            power = jnp.mean(mixed * mixed, 1, keepdims=True)
            out_ref[at, :] = (mixed * lax.rsqrt(power + 1e-05) * gain).astype(BF)


def shifted(value, axis, steps):
    count = lax.axis_size(axis)
    return lax.ppermute(value, axis, [(i, i + steps) for i in range(count - steps)])


def body(q_feat, k_feat, swa_query, swa_key, values, gain):
    tokens, columns = swa_query.shape
    heads = columns // HEAD_DIM
    width = q_feat.shape[1] // heads
    blocks = tokens // WINDOW
    feats = feature_rows(width)
    rows = state_rows(heads, width)
    halo_key = shifted(swa_key[tokens - WINDOW :], "seq", 1)
    halo_value = shifted(values[tokens - WINDOW :], "seq", 1)

    whole = lambda a: pl.BlockSpec(a.shape, lambda h: (0,) * a.ndim)
    vmem = pl.BlockSpec(memory_space=pltpu.VMEM)
    limit = pltpu.CompilerParams(vmem_limit_bytes=40 << 20)
    first, own = pl.pallas_call(
        functools.partial(state_kernel, heads=heads, width=width, blocks=blocks),
        out_shape=(jax.ShapeDtypeStruct((rows, HEAD_DIM), F32), jax.ShapeDtypeStruct((rows, HEAD_DIM), BF)),
        in_specs=[vmem] * 2,
        out_specs=(vmem, vmem),
        compiler_params=limit,
        cost_estimate=pl.CostEstimate(flops=2 * tokens * feats * columns, bytes_accessed=2 << 20, transcendentals=0),
        name="states",
    )(k_feat, values)

    prior = shifted(own, "seq", 1).astype(F32)
    running = own.astype(F32) + prior
    distance = 2
    count = lax.axis_size("seq")
    if count > 1:
        distance = 1
        prior = None
        running = own
        while distance < count:
            got = shifted(running.astype(BF), "seq", distance).astype(F32)
            prior = got if prior is None else prior + got
            running = running.astype(F32) + got
            distance *= 2

    col = pl.BlockSpec((tokens, HEAD_DIM), lambda h: (0, h))
    near = pl.BlockSpec((WINDOW, HEAD_DIM), lambda h: (0, h))
    phi_spec = pl.BlockSpec((heads, tokens, feats), lambda h: (0, 0, 0))
    big = jax.ShapeDtypeStruct((tokens, columns), F32)
    small = jax.ShapeDtypeStruct((WINDOW, columns), F32)
    num, den, win, total, top, phi = pl.pallas_call(
        functools.partial(local_kernel, width=width, blocks=blocks),
        grid=(heads,),
        out_shape=(big, big, big, small, small, jax.ShapeDtypeStruct((heads, tokens, feats), BF)),
        in_specs=[col, col, col, whole(q_feat), whole(k_feat)],
        out_specs=(col, col, col, near, near, phi_spec),
        compiler_params=limit,
        cost_estimate=pl.CostEstimate(flops=8 << 30, bytes_accessed=12 << 20, transcendentals=4 << 20),
        name="local",
    )(swa_query, swa_key, values, q_feat, k_feat)

    later = (lax.axis_index("seq") > 0).astype(jnp.int32).reshape(1)
    gain_row = gain.reshape(1, columns)
    state_spec = pl.BlockSpec((rows, HEAD_DIM), lambda h: (0, 0))
    return pl.pallas_call(
        functools.partial(final_kernel, heads=heads, width=width, blocks=blocks),
        grid=(heads,),
        out_shape=jax.ShapeDtypeStruct((tokens, columns), BF),
        in_specs=[
            pl.BlockSpec(memory_space=pltpu.SMEM),
            near, near, near, col, col, col, near, near,
            pl.BlockSpec((1, tokens, feats), lambda h: (h, 0, 0)),
            state_spec, state_spec,
            pl.BlockSpec((1, HEAD_DIM), lambda h: (0, h)),
        ],
        out_specs=col,
        compiler_params=limit,
        cost_estimate=pl.CostEstimate(flops=2 << 30, bytes_accessed=12 << 20, transcendentals=1 << 20),
        name="final",
    )(later, swa_query, halo_key, halo_value, num, den, win, total, top, phi, prior, first, gain_row)


def solution(mesh):
    tokens = P(("groups", "seq"), "head")
    return jax.shard_map(
        body, mesh=mesh, in_specs=(tokens,) * 5 + (P("head"),), out_specs=tokens, check_vma=False
    )
```

```python
import functools

import jax
import jax.numpy as jnp
from jax import lax
from jax.experimental import pallas as pl
from jax.experimental.pallas import tpu as pltpu
from jax.sharding import PartitionSpec as P

HEAD_DIM = 128
WINDOW = 512
TILE = 256
NEG = -1e30
SCALE = HEAD_DIM ** (-0.5) * 1.4426950408889634
BF = jnp.bfloat16
F32 = jnp.float32
GRANT = 16 << 20


def feature_rows(width):
    return -(-(width * (width + 1) // 2 + width + 1) // 16) * 16


def state_rows(heads, width):
    return heads * feature_rows(width) + 16


def nt(a, b):
    return lax.dot_general(a, b, (((1,), (1,)), ((), ())), preferred_element_type=F32)


def nn(a, b):
    return jnp.dot(a, b, preferred_element_type=F32)


def phi_rows(x, query):
    width, tokens = x.shape
    half = width // 2
    scale = 0.5**0.5 * width ** (-0.5)
    twice = jnp.concatenate([x, x], 0)
    rows = []
    for d in range(half):
        prod = ((x * twice[d : d + width]) * scale).astype(BF)
        if query and d:
            prod = prod * 2
        rows.append(prod)
    rows.append((x * width ** (-0.25)).astype(BF))
    cross = (x[:half] * x[half:]) * scale
    if query:
        cross = cross * 2
    pad = feature_rows(width) - (half * width + width + half)
    last = lax.broadcasted_iota(jnp.int32, (pad, tokens), 0)
    const = jnp.where(last == 0, 1.0, 0.0)
    rows.append(jnp.concatenate([cross, const], 0).astype(BF))
    return jnp.concatenate(rows, 0)


def with_ones(v):
    return jnp.concatenate([v, jnp.ones_like(v)], 1)


def lanes_of(h, count=1):
    return pl.ds(pl.multiple_of(h * HEAD_DIM, HEAD_DIM), count * HEAD_DIM)


def causal_masks():
    row = lax.broadcasted_iota(jnp.int32, (TILE, TILE), 0)
    col = lax.broadcasted_iota(jnp.int32, (TILE, TILE), 1)
    return col <= row, col > row


def prepare_kernel(kf_ref, q_ref, k_ref, v_ref, kv_ref, qb_ref, own_ref, first_ref, v_buf, sems, *, heads, width, blocks):
    feats = feature_rows(width)
    base = heads * feats
    tokens = v_buf.shape[0]
    ahead = heads // 2 * HEAD_DIM
    tail = pl.ds(tokens - WINDOW, WINDOW)
    copies = [
        pltpu.make_async_copy(v_ref, v_buf, sems.at[0]),
        pltpu.make_async_copy(k_ref.at[tail, :ahead], kv_ref.at[:WINDOW], sems.at[1]),
        pltpu.make_async_copy(v_ref.at[tail, :ahead], kv_ref.at[WINDOW:], sems.at[2]),
        pltpu.make_async_copy(q_ref.at[:WINDOW, ahead:], qb_ref, sems.at[3]),
    ]
    for copy in copies:
        copy.start()
    ones = jnp.ones((16, WINDOW), BF)
    first_ref[base:, :] = jnp.zeros((16, HEAD_DIM), F32)
    own_ref[base:, :] = jnp.zeros((16, HEAD_DIM), BF)
    copies[0].wait()
    for h in range(heads):
        phi = phi_rows(kf_ref[h * width : (h + 1) * width, :].astype(F32), False)
        total, norm = None, None
        for b in range(blocks):
            part = phi[:, b * WINDOW : (b + 1) * WINDOW]
            s = nn(part, v_buf[b * WINDOW : (b + 1) * WINDOW, h * HEAD_DIM : (h + 1) * HEAD_DIM])
            n = nt(ones, part)
            total = s if b == 0 else total + s
            norm = n if b == 0 else norm + n
            if b == 0:
                first_ref[h * feats : (h + 1) * feats, :] = s
                first_ref[base + 2 * h : base + 2 * h + 1, :] = n[:1, :HEAD_DIM]
                first_ref[base + 2 * h + 1 : base + 2 * h + 2, : feats - HEAD_DIM] = n[:1, HEAD_DIM:]
        own_ref[h * feats : (h + 1) * feats, :] = total.astype(BF)
        own_ref[base + 2 * h : base + 2 * h + 1, :] = norm[:1, :HEAD_DIM].astype(BF)
        own_ref[base + 2 * h + 1 : base + 2 * h + 2, : feats - HEAD_DIM] = norm[:1, HEAD_DIM:].astype(BF)
    for copy in copies[1:]:
        copy.wait()


def softmax_part(q, tiles):
    scores = []
    for key, _, mask in tiles:
        s = nt(q, key)
        scores.append(s if mask is None else jnp.where(mask, s, NEG))
    top = functools.reduce(jnp.maximum, scores)
    top = jnp.max(top, 1, keepdims=True)
    acc = None
    for s, (_, value, _) in zip(scores, tiles):
        p = jnp.exp2((s - top) * SCALE).astype(BF)
        part = nn(p, with_ones(value))
        acc = part if acc is None else acc + part
    return top, acc[:, :HEAD_DIM], acc[:, HEAD_DIM:]


def local_kernel(q_ref, k_ref, v_ref, qf_ref, kf_ref, num_ref, den_ref, win_ref, sum_ref, top_ref, phi_ref, *, start_head, width):
    causal, beyond = causal_masks()
    tokens = q_ref.shape[0]
    feats = feature_rows(width)

    def head(g, carry):
        h = g + start_head
        rows = pl.ds(pl.multiple_of(h * width, width), width)
        phi = phi_rows(qf_ref[rows, :].astype(F32), True).astype(F32).T.astype(BF)
        phi_ref[g] = phi
        kf = kf_ref[rows, :]
        kf = jnp.concatenate([kf, jnp.zeros((feats - HEAD_DIM - width, tokens), BF)], 0)
        for start in range(0, tokens, TILE):
            at = slice(start, start + TILE)
            tiles = []
            for back, mask in ((WINDOW, beyond), (WINDOW - TILE, None), (0, causal)):
                key_at = start - back
                if key_at >= 0:
                    ks = slice(key_at, key_at + TILE)
                    tiles.append((k_ref[ks, lanes_of(h)], v_ref[ks, lanes_of(h)], mask))
            top, out, total = softmax_part(q_ref[at, lanes_of(h)], tiles)
            if start >= WINDOW:
                win_ref[at, lanes_of(g)] = out / total
            else:
                win_ref[at, lanes_of(g)] = out
                sum_ref[at, lanes_of(g)] = total
                top_ref[at, lanes_of(g)] = jnp.broadcast_to(top, (TILE, HEAD_DIM))
            qf = phi[at, HEAD_DIM:]
            acc = None
            for key_at in range(start - start % WINDOW, start + TILE, TILE):
                ks = slice(key_at, key_at + TILE)
                r = nn(qf, kf[:, ks])
                half = width ** (-0.25)
                t = (r * (0.5 * half * half) + half) * r + 1.0
                if key_at == start:
                    t = jnp.where(causal, t, 0.0)
                part = nn(t.astype(BF), with_ones(v_ref[ks, lanes_of(h)]))
                acc = part if acc is None else acc + part
            num_ref[at, lanes_of(g)] = acc[:, :HEAD_DIM]
            den_ref[at, lanes_of(g)] = acc[:, HEAD_DIM:]
        return carry

    lax.fori_loop(0, num_ref.shape[1] // HEAD_DIM, head, 0)


def beyond_tiles(start, keys, values, beyond):
    tiles = []
    for key_at in range(start, WINDOW, TILE):
        ks = slice(key_at, key_at + TILE)
        tiles.append((keys(ks), values(ks), beyond if key_at == start else None))
    return tiles


def serve_kernel(qb_ref, k_ref, v_ref, out_ref, *, behind):
    _, beyond = causal_masks()
    base = k_ref.shape[0] - WINDOW
    count = qb_ref.shape[1] // HEAD_DIM
    lane = lax.broadcasted_iota(jnp.int32, (TILE, HEAD_DIM), 1)
    for start in range(0, WINDOW, TILE):
        at = slice(start, start + TILE)
        stats = jnp.zeros((TILE, HEAD_DIM), F32)
        for g in range(count):
            cols = slice((behind + g) * HEAD_DIM, (behind + g + 1) * HEAD_DIM)
            tiles = beyond_tiles(
                start,
                lambda ks: k_ref[base + ks.start : base + ks.stop, cols],
                lambda ks: v_ref[base + ks.start : base + ks.stop, cols],
                beyond,
            )
            top, out, total = softmax_part(qb_ref[at, g * HEAD_DIM : (g + 1) * HEAD_DIM], tiles)
            out_ref[at, g * HEAD_DIM : (g + 1) * HEAD_DIM] = out.astype(BF)
            stats = jnp.where(lane == g, top, stats)
            stats = jnp.where(lane == count + g, total, stats)
        stats = stats.T[: 2 * count]
        high = stats.astype(BF).astype(F32)
        middle = (stats - high).astype(BF).astype(F32)
        low = stats - high - middle
        pad = jnp.zeros((16 - 6 * count, TILE), F32)
        rows = jnp.concatenate([high, middle, low, pad], 0)
        line = WINDOW + start // TILE * 16
        out_ref[line : line + 16, :] = rows.astype(BF)


def final_kernel(later_ref, q_ref, kv_ref, ob_ref, *refs, heads, width, blocks):
    halves = [refs[:6], refs[6:12]]
    prior_ref, first_ref, gain_ref, out_ref = refs[12:]
    count = heads // 2
    feats = feature_rows(width)
    base = heads * feats
    _, beyond = causal_masks()

    def rhs(state, norm):
        wide = jnp.concatenate([jnp.broadcast_to(n, (HEAD_DIM, HEAD_DIM)) for n in norm], 1)
        cols = wide.T[:feats]
        return jnp.concatenate([state.astype(BF), cols.astype(BF)], 1)

    def one(g, part):
        h = g + part * count
        num_ref, den_ref, win_ref, sum_ref, top_ref, phi_ref = halves[part]
        rows = pl.ds(pl.multiple_of(h * feats, 16), feats)
        state = prior_ref[rows, :]
        norm = [prior_ref[pl.ds(base + 2 * h + i, 1), :] for i in range(2)]
        gain = gain_ref[:, lanes_of(h)]
        for b in range(blocks):
            if b == 1:
                state = state + first_ref[rows, :]
                norm = [n + first_ref[pl.ds(base + 2 * h + i, 1), :] for i, n in enumerate(norm)]
            both = rhs(state, norm)
            for start in range(b * WINDOW, (b + 1) * WINDOW, TILE):
                at = slice(start, start + TILE)
                lin = nn(phi_ref[g, at, :], both)
                mixed = (num_ref[at, lanes_of(g)] + lin[:, :HEAD_DIM]) / (den_ref[at, lanes_of(g)] + lin[:, HEAD_DIM:])
                window = win_ref[at, lanes_of(g)]
                if b == 0:
                    if part == 0:
                        tiles = beyond_tiles(
                            start,
                            lambda ks: kv_ref[ks, lanes_of(g)],
                            lambda ks: kv_ref[WINDOW + ks.start : WINDOW + ks.stop, lanes_of(g)],
                            beyond,
                        )
                        top, out, total = softmax_part(q_ref[at, lanes_of(h)], tiles)
                    else:
                        line = WINDOW + start // TILE * 16
                        stats = ob_ref[line : line + 16, :].astype(F32)
                        n = 2 * count
                        stats = stats[:n] + stats[n : 2 * n] + stats[2 * n : 3 * n]
                        stats = jnp.concatenate([stats, jnp.zeros((HEAD_DIM - n, TILE), F32)], 0).T
                        lane = lax.broadcasted_iota(jnp.int32, (TILE, HEAD_DIM), 1)
                        top = jnp.sum(jnp.where(lane == g, stats, 0.0), 1, keepdims=True)
                        total = jnp.sum(jnp.where(lane == count + g, stats, 0.0), 1, keepdims=True)
                        out = ob_ref[at, lanes_of(g)].astype(F32)
                    top = jnp.where(later_ref[0] > 0, top, 2 * NEG)
                    mine = top_ref[at, lanes_of(g)]
                    most = jnp.maximum(mine, top)
                    here = jnp.exp2((mine - most) * SCALE)
                    there = jnp.exp2((top - most) * SCALE)
                    window = (window * here + out * there) / (sum_ref[at, lanes_of(g)] * here + total * there)
                mixed = mixed + window
                power = jnp.mean(mixed * mixed, 1, keepdims=True)
                out_ref[at, lanes_of(h)] = (mixed * lax.rsqrt(power + 1e-05) * gain).astype(BF)

    def pair(g, carry):
        one(g, 0)
        one(g, 1)
        return carry

    lax.fori_loop(0, count, pair, 0)


def shifted(value, axis, steps):
    count = lax.axis_size(axis)
    pairs = [(i, i + steps) for i in range(count) if 0 <= i + steps < count]
    return lax.ppermute(value, axis, pairs)


def body(q_feat, k_feat, swa_query, swa_key, values, gain):
    tokens, columns = swa_query.shape
    heads = columns // HEAD_DIM
    half = heads // 2
    width = q_feat.shape[1] // heads
    blocks = tokens // WINDOW
    feats = feature_rows(width)
    rows = state_rows(heads, width)
    count = lax.axis_size("seq")
    vmem = pl.BlockSpec(memory_space=pltpu.VMEM)
    hbm = pl.BlockSpec(memory_space=pltpu.HBM)
    grant = pltpu.CompilerParams(vmem_limit_bytes=GRANT)
    qft, kft = q_feat.T, k_feat.T

    kv, qb, own, first = pl.pallas_call(
        functools.partial(prepare_kernel, heads=heads, width=width, blocks=blocks),
        out_shape=(
            jax.ShapeDtypeStruct((2 * WINDOW, half * HEAD_DIM), BF),
            jax.ShapeDtypeStruct((WINDOW, half * HEAD_DIM), BF),
            jax.ShapeDtypeStruct((rows, HEAD_DIM), BF),
            jax.ShapeDtypeStruct((rows, HEAD_DIM), F32),
        ),
        in_specs=[vmem, hbm, hbm, hbm],
        out_specs=(hbm, hbm, vmem, vmem),
        scratch_shapes=[pltpu.VMEM((tokens, columns), BF), pltpu.SemaphoreType.DMA((4,))],
        compiler_params=grant,
        cost_estimate=pl.CostEstimate(flops=1 << 30, bytes_accessed=3 << 20, transcendentals=0),
        name="prepare",
    )(kft, swa_query, swa_key, values)

    def local(start_head):
        wide = jax.ShapeDtypeStruct((tokens, half * HEAD_DIM), F32)
        near = jax.ShapeDtypeStruct((WINDOW, half * HEAD_DIM), F32)
        return pl.pallas_call(
            functools.partial(local_kernel, start_head=start_head, width=width),
            out_shape=(wide, wide, wide, near, near, jax.ShapeDtypeStruct((half, tokens, feats), BF)),
            in_specs=[vmem] * 5,
            out_specs=(vmem,) * 6,
            compiler_params=grant,
            cost_estimate=pl.CostEstimate(flops=4 << 30, bytes_accessed=6 << 20, transcendentals=2 << 20),
            name="local",
        )(swa_query, swa_key, values, qft, kft)

    if count <= 4:
        running, prior = own, None
        for i in range(count - 1):
            got = lax.ppermute(running, "seq", [(i, i + 1)])
            prior = got.astype(F32) if prior is None else prior + got.astype(F32)
            running = own + got
            if i == 0:
                halo = shifted(kv, "seq", 1)
                asked = shifted(qb, "seq", -1)
    else:
        running, prior, distance = own, None, 1
        halo = shifted(kv, "seq", 1)
        asked = shifted(qb, "seq", -1)
        while distance < count:
            got = shifted(running.astype(BF), "seq", distance).astype(F32)
            prior = got if prior is None else prior + got
            running = running.astype(F32) + got
            distance *= 2

    local_a = local(0)
    answer = pl.pallas_call(
        functools.partial(serve_kernel, behind=half),
        out_shape=jax.ShapeDtypeStruct((WINDOW + 16 * (WINDOW // TILE), half * HEAD_DIM), BF),
        in_specs=[vmem] * 3,
        out_specs=vmem,
        compiler_params=grant,
        cost_estimate=pl.CostEstimate(flops=1 << 30, bytes_accessed=2 << 20, transcendentals=1 << 19),
        name="serve",
    )(asked, swa_key, values)
    answered = shifted(answer, "seq", 1)
    local_b = local(half)

    later = (lax.axis_index("seq") > 0).astype(jnp.int32).reshape(1)
    return pl.pallas_call(
        functools.partial(final_kernel, heads=heads, width=width, blocks=blocks),
        out_shape=jax.ShapeDtypeStruct((tokens, columns), BF),
        in_specs=[pl.BlockSpec(memory_space=pltpu.SMEM)] + [vmem] * 18,
        out_specs=vmem,
        compiler_params=grant,
        cost_estimate=pl.CostEstimate(flops=2 << 30, bytes_accessed=12 << 20, transcendentals=1 << 20),
        name="final",
    )(later, swa_query, halo, answered, *local_a, *local_b, prior, first, gain.reshape(1, columns))


def solution(mesh):
    tokens = P(("groups", "seq"), "head")
    return jax.shard_map(
        body, mesh=mesh, in_specs=(tokens,) * 5 + (P("head"),), out_specs=tokens, check_vma=False
    )
```

```python
import functools

import jax
import jax.numpy as jnp
from jax import lax
from jax.experimental import pallas as pl
from jax.experimental.pallas import tpu as pltpu
from jax.sharding import PartitionSpec as P

HEAD_DIM = 128
WINDOW = 512
TILE = 256
NEG = -1e30
SCALE = HEAD_DIM ** (-0.5) * 1.4426950408889634
BF = jnp.bfloat16
F32 = jnp.float32
GRANT = 16 << 20


def feature_rows(width):
    return -(-(width * (width + 1) // 2 + width + 1) // 16) * 16


def state_rows(heads, width):
    return heads * feature_rows(width) + 16


def nt(a, b):
    return lax.dot_general(a, b, (((1,), (1,)), ((), ())), preferred_element_type=F32)


def nn(a, b):
    return jnp.dot(a, b, preferred_element_type=F32)


def phi_rows(x, query):
    width, tokens = x.shape
    half = width // 2
    scale = 0.5**0.5 * width ** (-0.5)
    twice = jnp.concatenate([x, x], 0)
    rows = []
    for d in range(half):
        prod = ((x * twice[d : d + width]) * scale).astype(BF)
        if query and d:
            prod = prod * 2
        rows.append(prod)
    rows.append((x * width ** (-0.25)).astype(BF))
    cross = (x[:half] * x[half:]) * scale
    if query:
        cross = cross * 2
    pad = feature_rows(width) - (half * width + width + half)
    last = lax.broadcasted_iota(jnp.int32, (pad, tokens), 0)
    const = jnp.where(last == 0, 1.0, 0.0)
    rows.append(jnp.concatenate([cross, const], 0).astype(BF))
    return jnp.concatenate(rows, 0)


def with_ones(v):
    return jnp.concatenate([v, jnp.ones_like(v)], 1)


def lanes_of(h, count=1):
    return pl.ds(pl.multiple_of(h * HEAD_DIM, HEAD_DIM), count * HEAD_DIM)


def causal_masks():
    row = lax.broadcasted_iota(jnp.int32, (TILE, TILE), 0)
    col = lax.broadcasted_iota(jnp.int32, (TILE, TILE), 1)
    return col <= row, col > row


def prepare_kernel(kf_ref, q_ref, k_ref, v_ref, kv_ref, qb_ref, own_ref, first_ref, v_buf, sems, *, heads, width, blocks):
    feats = feature_rows(width)
    base = heads * feats
    tokens = v_buf.shape[0]
    ahead = heads // 2 * HEAD_DIM
    tail = pl.ds(tokens - WINDOW, WINDOW)
    copies = [
        pltpu.make_async_copy(v_ref, v_buf, sems.at[0]),
        pltpu.make_async_copy(k_ref.at[tail, :ahead], kv_ref.at[:WINDOW], sems.at[1]),
        pltpu.make_async_copy(v_ref.at[tail, :ahead], kv_ref.at[WINDOW:], sems.at[2]),
        pltpu.make_async_copy(q_ref.at[:WINDOW, ahead:], qb_ref, sems.at[3]),
    ]
    for copy in copies:
        copy.start()
    ones = jnp.ones((16, WINDOW), BF)
    first_ref[base:, :] = jnp.zeros((16, HEAD_DIM), F32)
    own_ref[base:, :] = jnp.zeros((16, HEAD_DIM), BF)
    copies[0].wait()
    for h in range(heads):
        phi = phi_rows(kf_ref[h * width : (h + 1) * width, :].astype(F32), False)
        total, norm = None, None
        for b in range(blocks):
            part = phi[:, b * WINDOW : (b + 1) * WINDOW]
            s = nn(part, v_buf[b * WINDOW : (b + 1) * WINDOW, h * HEAD_DIM : (h + 1) * HEAD_DIM])
            n = nt(ones, part)
            total = s if b == 0 else total + s
            norm = n if b == 0 else norm + n
            if b == 0:
                first_ref[h * feats : (h + 1) * feats, :] = s
                first_ref[base + 2 * h : base + 2 * h + 1, :] = n[:1, :HEAD_DIM]
                first_ref[base + 2 * h + 1 : base + 2 * h + 2, : feats - HEAD_DIM] = n[:1, HEAD_DIM:]
        own_ref[h * feats : (h + 1) * feats, :] = total.astype(BF)
        own_ref[base + 2 * h : base + 2 * h + 1, :] = norm[:1, :HEAD_DIM].astype(BF)
        own_ref[base + 2 * h + 1 : base + 2 * h + 2, : feats - HEAD_DIM] = norm[:1, HEAD_DIM:].astype(BF)
    for copy in copies[1:]:
        copy.wait()


def softmax_part(q, tiles):
    scores = []
    for key, _, mask in tiles:
        s = nt(q, key)
        scores.append(s if mask is None else jnp.where(mask, s, NEG))
    top = functools.reduce(jnp.maximum, scores)
    top = jnp.max(top, 1, keepdims=True)
    acc = None
    for s, (_, value, _) in zip(scores, tiles):
        p = jnp.exp2((s - top) * SCALE).astype(BF)
        part = nn(p, with_ones(value))
        acc = part if acc is None else acc + part
    return top, acc[:, :HEAD_DIM], acc[:, HEAD_DIM:]


def local_kernel(q_ref, k_ref, v_ref, qf_ref, kf_ref, num_ref, den_ref, win_ref, sum_ref, top_ref, phi_ref, *, start_head, width):
    causal, beyond = causal_masks()
    tokens = q_ref.shape[0]
    feats = feature_rows(width)

    def head(g, carry):
        h = g + start_head
        rows = pl.ds(pl.multiple_of(h * width, width), width)
        phi = phi_rows(qf_ref[rows, :].astype(F32), True).astype(F32).T.astype(BF)
        phi_ref[g] = phi
        kf = kf_ref[rows, :]
        kf = jnp.concatenate([kf, jnp.zeros((feats - HEAD_DIM - width, tokens), BF)], 0)
        for start in range(0, tokens, TILE):
            at = slice(start, start + TILE)
            tiles = []
            for back, mask in ((WINDOW, beyond), (WINDOW - TILE, None), (0, causal)):
                key_at = start - back
                if key_at >= 0:
                    ks = slice(key_at, key_at + TILE)
                    tiles.append((k_ref[ks, lanes_of(h)], v_ref[ks, lanes_of(h)], mask))
            top, out, total = softmax_part(q_ref[at, lanes_of(h)], tiles)
            if start >= WINDOW:
                win_ref[at, lanes_of(g)] = out / total
            else:
                win_ref[at, lanes_of(g)] = out
                sum_ref[at, lanes_of(g)] = total
                top_ref[at, lanes_of(g)] = jnp.broadcast_to(top, (TILE, HEAD_DIM))
            qf = phi[at, HEAD_DIM:]
            acc = None
            for key_at in range(start - start % WINDOW, start + TILE, TILE):
                ks = slice(key_at, key_at + TILE)
                r = nn(qf, kf[:, ks])
                half = width ** (-0.25)
                t = (r * (0.5 * half * half) + half) * r + 1.0
                if key_at == start:
                    t = jnp.where(causal, t, 0.0)
                part = nn(t.astype(BF), with_ones(v_ref[ks, lanes_of(h)]))
                acc = part if acc is None else acc + part
            num_ref[at, lanes_of(g)] = acc[:, :HEAD_DIM]
            den_ref[at, lanes_of(g)] = acc[:, HEAD_DIM:]
        return carry

    lax.fori_loop(0, num_ref.shape[1] // HEAD_DIM, head, 0)


def beyond_tiles(start, keys, values, beyond):
    tiles = []
    for key_at in range(start, WINDOW, TILE):
        ks = slice(key_at, key_at + TILE)
        tiles.append((keys(ks), values(ks), beyond if key_at == start else None))
    return tiles


def serve_kernel(qb_ref, k_ref, v_ref, out_ref, *, behind):
    _, beyond = causal_masks()
    base = k_ref.shape[0] - WINDOW
    count = qb_ref.shape[1] // HEAD_DIM
    lane = lax.broadcasted_iota(jnp.int32, (TILE, HEAD_DIM), 1)
    for start in range(0, WINDOW, TILE):
        at = slice(start, start + TILE)
        stats = jnp.zeros((TILE, HEAD_DIM), F32)
        for g in range(count):
            cols = slice((behind + g) * HEAD_DIM, (behind + g + 1) * HEAD_DIM)
            tiles = beyond_tiles(
                start,
                lambda ks: k_ref[base + ks.start : base + ks.stop, cols],
                lambda ks: v_ref[base + ks.start : base + ks.stop, cols],
                beyond,
            )
            top, out, total = softmax_part(qb_ref[at, g * HEAD_DIM : (g + 1) * HEAD_DIM], tiles)
            out_ref[at, g * HEAD_DIM : (g + 1) * HEAD_DIM] = out.astype(BF)
            stats = jnp.where(lane == g, top, stats)
            stats = jnp.where(lane == count + g, total, stats)
        stats = stats.T[: 2 * count]
        high = stats.astype(BF).astype(F32)
        middle = (stats - high).astype(BF).astype(F32)
        low = stats - high - middle
        pad = jnp.ones((16 - 6 * count, TILE), F32)
        rows = jnp.concatenate([high, middle, low, pad], 0)
        line = WINDOW + start // TILE * 16
        out_ref[line : line + 16, :] = rows.astype(BF)


def final_kernel(q_ref, kv_ref, ob_ref, *refs, heads, width, blocks):
    halves = [refs[:6], refs[6:12]]
    *prior_refs, first_ref, gain_ref, out_ref = refs[12:]
    count = heads // 2
    feats = feature_rows(width)
    base = heads * feats
    _, beyond = causal_masks()

    def rhs(state, norm):
        wide = jnp.concatenate([jnp.broadcast_to(n, (HEAD_DIM, HEAD_DIM)) for n in norm], 1)
        cols = wide.T[:feats]
        return jnp.concatenate([state.astype(BF), cols.astype(BF)], 1)

    later = ob_ref[WINDOW + 15 : WINDOW + 16, :1].astype(F32) > 0
    tail = functools.reduce(jnp.add, [ref[base:, :].astype(F32) for ref in prior_refs])
    line_of = lax.broadcasted_iota(jnp.int32, (16, HEAD_DIM), 0)

    def one(g, part):
        h = g + part * count
        tails = [jnp.sum(jnp.where(line_of == 2 * h + i, tail, 0.0), 0, keepdims=True) for i in range(2)]
        num_ref, den_ref, win_ref, sum_ref, top_ref, phi_ref = halves[part]
        rows = pl.ds(pl.multiple_of(h * feats, 16), feats)
        state = functools.reduce(jnp.add, [ref[rows, :].astype(F32) for ref in prior_refs])
        norm = [tails[0], tails[1]]
        gain = gain_ref[:, lanes_of(h)]
        for b in range(blocks):
            if b == 1:
                state = state + first_ref[rows, :]
                norm = [n + first_ref[pl.ds(base + 2 * h + i, 1), :] for i, n in enumerate(norm)]
            both = rhs(state, norm)
            for start in range(b * WINDOW, (b + 1) * WINDOW, TILE):
                at = slice(start, start + TILE)
                lin = nn(phi_ref[g, at, :], both)
                mixed = (num_ref[at, lanes_of(g)] + lin[:, :HEAD_DIM]) / (den_ref[at, lanes_of(g)] + lin[:, HEAD_DIM:])
                window = win_ref[at, lanes_of(g)]
                if b == 0:
                    if part == 0:
                        tiles = beyond_tiles(
                            start,
                            lambda ks: kv_ref[ks, lanes_of(g)],
                            lambda ks: kv_ref[WINDOW + ks.start : WINDOW + ks.stop, lanes_of(g)],
                            beyond,
                        )
                        top, out, total = softmax_part(q_ref[at, lanes_of(h)], tiles)
                    else:
                        line = WINDOW + start // TILE * 16
                        stats = ob_ref[line : line + 16, :].astype(F32)
                        n = 2 * count
                        stats = stats[:n] + stats[n : 2 * n] + stats[2 * n : 3 * n]
                        stats = jnp.concatenate([stats, jnp.zeros((HEAD_DIM - n, TILE), F32)], 0).T
                        lane = lax.broadcasted_iota(jnp.int32, (TILE, HEAD_DIM), 1)
                        top = jnp.sum(jnp.where(lane == g, stats, 0.0), 1, keepdims=True)
                        total = jnp.sum(jnp.where(lane == count + g, stats, 0.0), 1, keepdims=True)
                        out = ob_ref[at, lanes_of(g)].astype(F32)
                    top = jnp.where(later, top, 2 * NEG)
                    mine = top_ref[at, lanes_of(g)]
                    most = jnp.maximum(mine, top)
                    here = jnp.exp2((mine - most) * SCALE)
                    there = jnp.exp2((top - most) * SCALE)
                    window = (window * here + out * there) / (sum_ref[at, lanes_of(g)] * here + total * there)
                mixed = mixed + window
                power = jnp.mean(mixed * mixed, 1, keepdims=True)
                out_ref[at, lanes_of(h)] = (mixed * lax.rsqrt(power + 1e-05) * gain).astype(BF)

    def pair(g, carry):
        one(g, 0)
        one(g, 1)
        return carry

    lax.fori_loop(0, count, pair, 0)


def shifted(value, axis, steps):
    count = lax.axis_size(axis)
    pairs = [(i, i + steps) for i in range(count) if 0 <= i + steps < count]
    return lax.ppermute(value, axis, pairs)


def body(q_feat, k_feat, swa_query, swa_key, values, gain):
    tokens, columns = swa_query.shape
    heads = columns // HEAD_DIM
    half = heads // 2
    width = q_feat.shape[1] // heads
    blocks = tokens // WINDOW
    feats = feature_rows(width)
    rows = state_rows(heads, width)
    count = lax.axis_size("seq")
    vmem = pl.BlockSpec(memory_space=pltpu.VMEM)
    hbm = pl.BlockSpec(memory_space=pltpu.HBM)
    grant = pltpu.CompilerParams(vmem_limit_bytes=GRANT)
    qft, kft = q_feat.T, k_feat.T

    kv, qb, own, first = pl.pallas_call(
        functools.partial(prepare_kernel, heads=heads, width=width, blocks=blocks),
        out_shape=(
            jax.ShapeDtypeStruct((2 * WINDOW, half * HEAD_DIM), BF),
            jax.ShapeDtypeStruct((WINDOW, half * HEAD_DIM), BF),
            jax.ShapeDtypeStruct((rows, HEAD_DIM), BF),
            jax.ShapeDtypeStruct((rows, HEAD_DIM), F32),
        ),
        in_specs=[vmem, hbm, hbm, hbm],
        out_specs=(hbm, hbm, vmem, vmem),
        scratch_shapes=[pltpu.VMEM((tokens, columns), BF), pltpu.SemaphoreType.DMA((4,))],
        compiler_params=grant,
        cost_estimate=pl.CostEstimate(flops=1 << 30, bytes_accessed=3 << 20, transcendentals=0),
        name="prepare",
    )(kft, *[pltpu.with_memory_space_constraint(a, pltpu.HBM) for a in (swa_query, swa_key, values)])

    def local(start_head):
        wide = jax.ShapeDtypeStruct((tokens, half * HEAD_DIM), F32)
        near = jax.ShapeDtypeStruct((WINDOW, half * HEAD_DIM), F32)
        return pl.pallas_call(
            functools.partial(local_kernel, start_head=start_head, width=width),
            out_shape=(wide, wide, wide, near, near, jax.ShapeDtypeStruct((half, tokens, feats), BF)),
            in_specs=[vmem] * 5,
            out_specs=(vmem,) * 6,
            compiler_params=grant,
            cost_estimate=pl.CostEstimate(flops=4 << 30, bytes_accessed=6 << 20, transcendentals=2 << 20),
            name="local",
        )(swa_query, swa_key, values, qft, kft)

    if count <= 4:
        running, prior = own, []
        for i in range(count - 1):
            got = lax.ppermute(running, "seq", [(i, i + 1)])
            prior.append(got)
            running = own + got
            if i == 0:
                halo = shifted(kv, "seq", 1)
                asked = shifted(qb, "seq", -1)
    else:
        running, prior, distance = own, [], 1
        halo = shifted(kv, "seq", 1)
        asked = shifted(qb, "seq", -1)
        while distance < count:
            got = shifted(running, "seq", distance)
            prior.append(got)
            running = running + got
            distance *= 2

    local_a = local(0)
    answer = pl.pallas_call(
        functools.partial(serve_kernel, behind=half),
        out_shape=jax.ShapeDtypeStruct((WINDOW + 16 * (WINDOW // TILE), half * HEAD_DIM), BF),
        in_specs=[vmem] * 3,
        out_specs=vmem,
        compiler_params=grant,
        cost_estimate=pl.CostEstimate(flops=1 << 30, bytes_accessed=2 << 20, transcendentals=1 << 19),
        name="serve",
    )(asked, swa_key, values)
    answered = shifted(answer, "seq", 1)
    local_b = local(half)

    return pl.pallas_call(
        functools.partial(final_kernel, heads=heads, width=width, blocks=blocks),
        out_shape=jax.ShapeDtypeStruct((tokens, columns), BF),
        in_specs=[vmem] * (17 + len(prior)),
        out_specs=vmem,
        compiler_params=grant,
        cost_estimate=pl.CostEstimate(flops=2 << 30, bytes_accessed=12 << 20, transcendentals=1 << 20),
        name="final",
    )(swa_query, halo, answered, *local_a, *local_b, *prior, first, gain.reshape(1, columns))


def solution(mesh):
    tokens = P(("groups", "seq"), "head")
    return jax.shard_map(
        body, mesh=mesh, in_specs=(tokens,) * 5 + (P("head"),), out_specs=tokens, check_vma=False
    )
```

```python
import functools

import jax
import jax.numpy as jnp
from jax import lax
from jax.experimental import pallas as pl
from jax.experimental.pallas import tpu as pltpu
from jax.sharding import PartitionSpec as P

HEAD_DIM = 128
WINDOW = 512
TILE = 256
NEG = -1e30
SCALE = HEAD_DIM ** (-0.5) * 1.4426950408889634
BF = jnp.bfloat16
F32 = jnp.float32
GRANT = 16 << 20
LA = 1 << 30
LB = 4 << 30
SV = 1 << 30
PR = 1 << 30
RL = 1 << 17


def feature_rows(width):
    return -(-(width * (width + 1) // 2 + width + 1) // 16) * 16


def state_rows(heads, width):
    return heads * feature_rows(width) + 16


def nt(a, b):
    return lax.dot_general(a, b, (((1,), (1,)), ((), ())), preferred_element_type=F32)


def nn(a, b):
    return jnp.dot(a, b, preferred_element_type=F32)


def phi_rows(x, query):
    width, tokens = x.shape
    half = width // 2
    scale = 0.5**0.5 * width ** (-0.5)
    twice = jnp.concatenate([x, x], 0)
    rows = []
    for d in range(half):
        prod = ((x * twice[d : d + width]) * scale).astype(BF)
        if query and d:
            prod = prod * 2
        rows.append(prod)
    rows.append((x * width ** (-0.25)).astype(BF))
    cross = (x[:half] * x[half:]) * scale
    if query:
        cross = cross * 2
    pad = feature_rows(width) - (half * width + width + half)
    last = lax.broadcasted_iota(jnp.int32, (pad, tokens), 0)
    const = jnp.where(last == 0, 1.0, 0.0)
    rows.append(jnp.concatenate([cross, const], 0).astype(BF))
    return jnp.concatenate(rows, 0)


def with_ones(v):
    return jnp.concatenate([v, jnp.ones_like(v)], 1)


def lanes_of(h, count=1):
    return pl.ds(pl.multiple_of(h * HEAD_DIM, HEAD_DIM), count * HEAD_DIM)


def causal_masks():
    row = lax.broadcasted_iota(jnp.int32, (TILE, TILE), 0)
    col = lax.broadcasted_iota(jnp.int32, (TILE, TILE), 1)
    return col <= row, col > row


def prepare_kernel(kf_hbm, q_hbm, k_hbm, v_hbm, kp_ref, vp_ref, qb_ref, own_ref, before_ref, kf_ref, v_ref, sems, *, heads, width):
    feats = feature_rows(width)
    base = heads * feats
    tokens = v_ref.shape[0]
    ahead = heads // 2 * HEAD_DIM
    tail = pl.ds(tokens - WINDOW, WINDOW)
    copies = [
        pltpu.make_async_copy(kf_hbm, kf_ref, sems.at[0]),
        pltpu.make_async_copy(v_hbm, v_ref, sems.at[1]),
        pltpu.make_async_copy(k_hbm.at[tail, :ahead], kp_ref, sems.at[2]),
        pltpu.make_async_copy(v_hbm.at[tail, :ahead], vp_ref, sems.at[3]),
        pltpu.make_async_copy(q_hbm.at[:WINDOW, ahead:], qb_ref, sems.at[4]),
    ]
    for copy in copies:
        copy.start()
    ones = jnp.ones((16, tokens), BF)
    own_ref[base:, :] = jnp.zeros((16, HEAD_DIM), BF)
    copies[0].wait()
    copies[1].wait()
    for h in range(heads):
        phi = phi_rows(kf_ref[h * width : (h + 1) * width, :].astype(F32), False)
        total = None
        for t in range(tokens // TILE):
            at = slice(t * TILE, (t + 1) * TILE)
            s = nn(phi[:, at], with_ones(v_ref[at, h * HEAD_DIM : (h + 1) * HEAD_DIM]))
            total = s if t == 0 else total + s
            if t < tokens // TILE - 1:
                before_ref[t, h * feats : (h + 1) * feats, :] = total
        norm = nt(ones, phi)
        own_ref[h * feats : (h + 1) * feats, :] = total[:, :HEAD_DIM].astype(BF)
        own_ref[base + 2 * h : base + 2 * h + 1, :] = norm[:1, :HEAD_DIM].astype(BF)
        own_ref[base + 2 * h + 1 : base + 2 * h + 2, : feats - HEAD_DIM] = norm[:1, HEAD_DIM:].astype(BF)
    for copy in copies[2:]:
        copy.wait()
    top = kp_ref[:16, :]
    row = lax.broadcasted_iota(jnp.int32, top.shape, 0)
    kp_ref[:16, :] = jnp.where(row == 0, jnp.ones((), BF), top)


def softmax_parts(jobs, ahead=2):
    scores = []
    for i in range(len(jobs)):
        while len(scores) < min(len(jobs), i + 1 + ahead):
            query, key = jobs[len(scores)][:2]
            scores.append(nt(query(), key()))
        _, _, value, first, last, use = jobs[i]
        s, scores[i] = scores[i], None
        parts = [s[:, at : at + TILE] for at in range(0, s.shape[1], TILE)]
        if first is not None:
            parts[0] = jnp.where(first, parts[0], NEG)
        if last is not None:
            parts[-1] = jnp.where(last, parts[-1], NEG)
        top = jnp.max(functools.reduce(jnp.maximum, parts), 1, keepdims=True)
        p = jnp.concatenate([jnp.exp2((part - top) * SCALE).astype(BF) for part in parts], 1)
        acc = nn(p, with_ones(value()))
        use(top, acc[:, :HEAD_DIM], acc[:, HEAD_DIM:])


def local_kernel(q_ref, k_ref, v_ref, qf_ref, kf_ref, num_ref, den_ref, win_ref, sum_ref, top_ref, phi_ref, *, start_head, width):
    causal, beyond = causal_masks()
    tokens = q_ref.shape[0]
    feats = feature_rows(width)

    jobs = []

    def job(g, start):
        h = g + start_head
        at = slice(start, start + TILE)
        keys = slice(max(0, start - WINDOW), start + TILE)
        lanes = slice(g * HEAD_DIM, (g + 1) * HEAD_DIM)
        wide = slice(h * HEAD_DIM, (h + 1) * HEAD_DIM)

        def use(top, out, total):
            if start >= WINDOW:
                win_ref[at, lanes] = out / total
            else:
                win_ref[at, lanes] = out
                sum_ref[at, lanes] = total
                top_ref[at, lanes] = jnp.broadcast_to(top, (TILE, HEAD_DIM))
            r = nn(phi_ref[g, at, HEAD_DIM:], kfs[g][:, at])
            part = width ** (-0.25)
            t = jnp.where(causal, (r * (0.5 * part * part) + part) * r + 1.0, 0.0)
            both = nn(t.astype(BF), with_ones(v_ref[at, wide]))
            num_ref[at, lanes] = both[:, :HEAD_DIM]
            den_ref[at, lanes] = both[:, HEAD_DIM:]

        first = beyond if start >= WINDOW else None
        jobs.append((lambda: q_ref[at, wide], lambda: k_ref[keys, wide], lambda: v_ref[keys, wide], first, causal, use))

    kfs = []
    for g in range(num_ref.shape[1] // HEAD_DIM):
        h = g + start_head
        rows = slice(h * width, (h + 1) * width)
        phi_ref[g] = phi_rows(qf_ref[rows, :].astype(F32), True).astype(F32).T.astype(BF)
        kfs.append(jnp.concatenate([kf_ref[rows, :], jnp.zeros((feats - HEAD_DIM - width, tokens), BF)], 0))
        for start in range(0, tokens, TILE):
            job(g, start)
    softmax_parts(jobs)


def serve_kernel(qb_ref, k_ref, v_ref, out_ref, *, behind):
    _, beyond = causal_masks()
    base = k_ref.shape[0] - WINDOW
    count = qb_ref.shape[1] // HEAD_DIM
    lane = lax.broadcasted_iota(jnp.int32, (TILE, HEAD_DIM), 1)
    jobs = []
    stats = [jnp.zeros((TILE, HEAD_DIM), F32) for _ in range(WINDOW // TILE)]

    def job(start, g):
        at = slice(start, start + TILE)
        keys = slice(base + start, base + WINDOW)
        lanes = slice(g * HEAD_DIM, (g + 1) * HEAD_DIM)
        wide = slice((behind + g) * HEAD_DIM, (behind + g + 1) * HEAD_DIM)

        def use(top, out, total):
            out_ref[at, lanes] = out.astype(BF)
            stat = jnp.where(lane == g, top, stats[start // TILE])
            stats[start // TILE] = jnp.where(lane == count + g, total, stat)

        jobs.append((lambda: qb_ref[at, lanes], lambda: k_ref[keys, wide], lambda: v_ref[keys, wide], beyond, None, use))

    for start in range(0, WINDOW, TILE):
        for g in range(count):
            job(start, g)
    softmax_parts(jobs)
    for i, stat in enumerate(stats):
        stat = stat.T[: 2 * count]
        high = stat.astype(BF).astype(F32)
        middle = (stat - high).astype(BF).astype(F32)
        low = stat - high - middle
        pad = jnp.ones((16 - 6 * count, TILE), F32)
        rows = jnp.concatenate([high, middle, low, pad], 0)
        out_ref[WINDOW + 16 * i : WINDOW + 16 * (i + 1), :] = rows.astype(BF)


def merged(window, mine, total, top, out, count, later):
    top = jnp.where(later, top, 2 * NEG)
    most = jnp.maximum(mine, top)
    here = jnp.exp2((mine - most) * SCALE)
    there = jnp.exp2((top - most) * SCALE)
    return (window * here + out * there) / (total * here + count * there)


def normed(mixed, gain):
    power = jnp.mean(mixed * mixed, 1, keepdims=True)
    return (mixed * lax.rsqrt(power + 1e-05) * gain).astype(BF)


def first_final_kernel(q_ref, kp_ref, vp_ref, *refs, heads, width):
    halves = [refs[:6], refs[6:10]]
    *prior_refs, before_ref, gain_hbm, out_hbm, lin_ref, gain_b_ref, gain_ref, near_ref, out_ref, sems = refs[10:]
    count = heads // 2
    tokens = q_ref.shape[0]
    feats = feature_rows(width)
    base = heads * feats
    fetch = pltpu.make_async_copy(gain_hbm, gain_ref, sems.at[heads])
    fetch.start()
    _, beyond = causal_masks()
    later = kp_ref[:1, :1].astype(F32) > 0
    jobs = []

    def job(g, start):
        at = slice(start, start + TILE)
        keys = slice(start, WINDOW)
        cols = slice(g * HEAD_DIM, (g + 1) * HEAD_DIM)
        win_ref, _, sum_ref, top_ref = halves[0][2:]

        def use(top, out, total):
            near_ref[at, cols] = merged(win_ref[at, cols], top_ref[at, cols], sum_ref[at, cols], top, out, total, later)

        jobs.append((lambda: q_ref[at, cols], lambda: kp_ref[keys, cols], lambda: vp_ref[keys, cols], beyond, None, use))

    for g in range(count):
        for start in range(0, WINDOW, TILE):
            job(g, start)

    def prior(rows):
        return functools.reduce(jnp.add, [ref[rows, :].astype(F32) for ref in prior_refs])

    tail = jnp.concatenate([prior(slice(base, base + 16)), jnp.zeros((HEAD_DIM - 16, HEAD_DIM), F32)], 0).T

    def state(h):
        norm = [
            jnp.broadcast_to(tail[:, 2 * h : 2 * h + 1], (HEAD_DIM, HEAD_DIM)),
            jnp.broadcast_to(tail[: feats - HEAD_DIM, 2 * h + 1 : 2 * h + 2], (feats - HEAD_DIM, HEAD_DIM)),
        ]
        return jnp.concatenate([prior(slice(h * feats, (h + 1) * feats)), jnp.concatenate(norm, 0)], 1)

    softmax_parts(jobs)
    order = [(h, start) for h in list(range(count, heads)) + list(range(count)) for start in range(0, tokens, TILE)]
    states, lins, copies = {}, [], []
    for i, (h, start) in enumerate(order):
        while len(lins) < min(len(order), i + 2):
            hn, sn = order[len(lins)]
            rows = slice(hn * feats, (hn + 1) * feats)
            if hn not in states:
                states[hn] = state(hn)
            both = states[hn] if sn == 0 else states[hn] + before_ref[sn // TILE - 1, rows, :]
            lins.append(nn(halves[hn // count][3][hn % count, sn : sn + TILE, :], both.astype(BF)))
        lin, lins[i] = lins[i], None
        part, g = h // count, h % count
        num_ref, den_ref, win_ref = halves[part][:3]
        at = slice(start, start + TILE)
        cols = slice(g * HEAD_DIM, (g + 1) * HEAD_DIM)
        wide = slice(h * HEAD_DIM, (h + 1) * HEAD_DIM)
        mixed = (num_ref[at, cols] + lin[:, :HEAD_DIM]) / (den_ref[at, cols] + lin[:, HEAD_DIM:])
        if start < WINDOW and part == 1:
            lin_ref[at, cols] = mixed
        else:
            if not copies and start == WINDOW:
                fetch.wait()
                gain_b_ref[...] = gain_ref[:, count * HEAD_DIM :]
            window = near_ref[at, cols] if start < WINDOW else win_ref[at, cols]
            out_ref[at, wide] = normed(mixed + window, gain_ref[:, wide])
        if start + TILE == tokens:
            area = (pl.ds(WINDOW * part, tokens - WINDOW * part), pl.ds(h * HEAD_DIM, HEAD_DIM))
            copies.append(pltpu.make_async_copy(out_ref.at[area], out_hbm.at[area], sems.at[h]))
            copies[-1].start()
    for copy in copies:
        copy.wait()


def last_final_kernel(ob_ref, lin_ref, win_ref, sum_ref, top_ref, gain_ref, _, out_hbm, out_ref, sems):
    count = lin_ref.shape[1] // HEAD_DIM
    ahead = out_hbm.shape[1] - count * HEAD_DIM
    later = ob_ref[WINDOW + 15 : WINDOW + 16, :1].astype(F32) > 0
    copies = []
    stats = []
    for i in range(WINDOW // TILE):
        got = ob_ref[WINDOW + 16 * i : WINDOW + 16 * (i + 1), :].astype(F32)
        n = 2 * count
        got = got[:n] + got[n : 2 * n] + got[2 * n : 3 * n]
        stats.append(jnp.concatenate([got, jnp.zeros((HEAD_DIM - n, TILE), F32)], 0).T)
    for start in range(0, WINDOW, TILE):
        at = slice(start, start + TILE)
        stat = stats[start // TILE]
        for g in range(count):
            cols = slice(g * HEAD_DIM, (g + 1) * HEAD_DIM)
            out = ob_ref[at, cols].astype(F32)
            window = merged(win_ref[at, cols], top_ref[at, cols], sum_ref[at, cols], stat[:, g : g + 1], out, stat[:, count + g : count + g + 1], later)
            out_ref[at, cols] = normed(lin_ref[at, cols] + window, gain_ref[:, cols])
        copy = pltpu.make_async_copy(out_ref.at[at, :], out_hbm.at[at, ahead:], sems.at[start // TILE])
        copy.start()
        copies.append(copy)
    for copy in copies:
        copy.wait()


def relay_kernel(own_ref, got_ref, _, sum_ref, pass_ref):
    sum_ref[...] = own_ref[...] + got_ref[...]


def shifted(value, axis, steps):
    count = lax.axis_size(axis)
    pairs = [(i, i + steps) for i in range(count) if 0 <= i + steps < count]
    return lax.ppermute(value, axis, pairs)


def body(q_feat, k_feat, swa_query, swa_key, values, gain):
    tokens, columns = swa_query.shape
    heads = columns // HEAD_DIM
    half = heads // 2
    width = q_feat.shape[1] // heads
    feats = feature_rows(width)
    rows = state_rows(heads, width)
    count = lax.axis_size("seq")
    vmem = pl.BlockSpec(memory_space=pltpu.VMEM)
    hbm = pl.BlockSpec(memory_space=pltpu.HBM)
    grant = pltpu.CompilerParams(vmem_limit_bytes=GRANT)
    qft, kft = q_feat.T, k_feat.T

    in_hbm = lambda *arrays: [pltpu.with_memory_space_constraint(a, pltpu.HBM) for a in arrays]
    kp, vp, qb, own, before = pl.pallas_call(
        functools.partial(prepare_kernel, heads=heads, width=width),
        out_shape=(
            jax.ShapeDtypeStruct((WINDOW, half * HEAD_DIM), BF),
            jax.ShapeDtypeStruct((WINDOW, half * HEAD_DIM), BF),
            jax.ShapeDtypeStruct((WINDOW, half * HEAD_DIM), BF),
            jax.ShapeDtypeStruct((rows, HEAD_DIM), BF),
            jax.ShapeDtypeStruct((tokens // TILE - 1, heads * feats, 2 * HEAD_DIM), F32),
        ),
        in_specs=[hbm] * 4,
        out_specs=(vmem,) * 5,
        scratch_shapes=[
            pltpu.VMEM(kft.shape, BF),
            pltpu.VMEM((tokens, columns), BF),
            pltpu.SemaphoreType.DMA((5,)),
        ],
        compiler_params=grant,
        cost_estimate=pl.CostEstimate(flops=1 << 30, bytes_accessed=3 << 20, transcendentals=0),
        name="prepare",
    )(*in_hbm(kft, swa_query, swa_key, values))

    def local(start_head, flops):
        wide = jax.ShapeDtypeStruct((tokens, half * HEAD_DIM), F32)
        near = jax.ShapeDtypeStruct((WINDOW, half * HEAD_DIM), F32)
        return pl.pallas_call(
            functools.partial(local_kernel, start_head=start_head, width=width),
            out_shape=(wide, wide, wide, near, near, jax.ShapeDtypeStruct((half, tokens, feats), BF)),
            in_specs=[vmem] * 5,
            out_specs=(vmem,) * 6,
            compiler_params=grant,
            cost_estimate=pl.CostEstimate(flops=flops, bytes_accessed=1 << 20, transcendentals=1 << 10),
            name="local",
        )(swa_query, swa_key, values, qft, kft)

    if count <= 4:
        running, prior = own, []
        for i in range(count - 1):
            got = lax.ppermute(running, "seq", [(i, i + 1)])
            prior.append(got)
            running = own + got
            if i == 0:
                asked = shifted(qb, "seq", -1)
                running, vp = pl.pallas_call(
                    relay_kernel,
                    out_shape=(jax.ShapeDtypeStruct(own.shape, BF), jax.ShapeDtypeStruct(vp.shape, BF)),
                    in_specs=[vmem] * 3,
                    out_specs=(vmem,) * 2,
                    input_output_aliases={2: 1},
                    compiler_params=grant,
                    cost_estimate=pl.CostEstimate(flops=RL, bytes_accessed=1 << 19, transcendentals=0),
                    name="relay",
                )(own, got, vp)
                halo = shifted(kp, "seq", 1), shifted(vp, "seq", 1)
    else:
        running, prior, distance = own, [], 1
        halo = shifted(kp, "seq", 1), shifted(vp, "seq", 1)
        asked = shifted(qb, "seq", -1)
        while distance < count:
            got = shifted(running, "seq", distance)
            prior.append(got)
            running = running + got
            distance *= 2

    local_a = local(0, LA)
    answer = pl.pallas_call(
        functools.partial(serve_kernel, behind=half),
        out_shape=jax.ShapeDtypeStruct((WINDOW + 16 * (WINDOW // TILE), half * HEAD_DIM), BF),
        in_specs=[vmem] * 3,
        out_specs=vmem,
        compiler_params=grant,
        cost_estimate=pl.CostEstimate(flops=SV, bytes_accessed=1 << 20, transcendentals=1 << 10),
        name="serve",
    )(asked, swa_key, values)
    answered = shifted(answer, "seq", 1)
    local_b = local(half, LB)

    num_a, den_a, win_a, sum_a, top_a, phi_a = local_a
    num_b, den_b, win_b, sum_b, top_b, phi_b = local_b
    gain_row = in_hbm(gain.reshape(1, columns))
    operands = (swa_query, *halo, num_a, den_a, win_a, phi_a, sum_a, top_a, num_b, den_b, win_b, phi_b, *prior, before)
    out, lin, gain_b = pl.pallas_call(
        functools.partial(first_final_kernel, heads=heads, width=width),
        out_shape=(
            jax.ShapeDtypeStruct((tokens, columns), BF),
            jax.ShapeDtypeStruct((WINDOW, half * HEAD_DIM), F32),
            jax.ShapeDtypeStruct((1, half * HEAD_DIM), F32),
        ),
        in_specs=[vmem] * len(operands) + [hbm],
        out_specs=(hbm, vmem, vmem),
        scratch_shapes=[
            pltpu.VMEM((1, columns), F32),
            pltpu.VMEM((WINDOW, half * HEAD_DIM), F32),
            pltpu.VMEM((tokens, columns), BF),
            pltpu.SemaphoreType.DMA((heads + 1,)),
        ],
        compiler_params=grant,
        cost_estimate=pl.CostEstimate(flops=2 << 30, bytes_accessed=12 << 20, transcendentals=1 << 20),
        name="final",
    )(*operands, *gain_row)
    return pl.pallas_call(
        last_final_kernel,
        out_shape=jax.ShapeDtypeStruct((tokens, columns), BF),
        in_specs=[vmem] * 6 + [hbm],
        out_specs=hbm,
        scratch_shapes=[
            pltpu.VMEM((WINDOW, half * HEAD_DIM), BF),
            pltpu.SemaphoreType.DMA((WINDOW // TILE,)),
        ],
        input_output_aliases={6: 0},
        compiler_params=grant,
        cost_estimate=pl.CostEstimate(flops=1 << 20, bytes_accessed=3 << 20, transcendentals=1 << 19),
        name="last",
    )(answered, lin, win_b, sum_b, top_b, gain_b, out)


def solution(mesh):
    tokens = P(("groups", "seq"), "head")
    return jax.shard_map(
        body, mesh=mesh, in_specs=(tokens,) * 5 + (P("head"),), out_specs=tokens, check_vma=False
    )
```

```python
import functools

import jax
import jax.numpy as jnp
from jax import lax
from jax.experimental import pallas as pl
from jax.experimental.pallas import tpu as pltpu
from jax.sharding import PartitionSpec as P

HEAD_DIM = 128
WINDOW = 512
TILE = 256
NEG = -1e30
SCALE = HEAD_DIM ** (-0.5) * 1.4426950408889634
BF = jnp.bfloat16
F32 = jnp.float32
GRANT = 16 << 20
LA = 1 << 30
LB = 4 << 30
SV = 1 << 30
PR = 1 << 30
RL = 1 << 17
FN = 2 << 30


def feature_rows(width):
    return -(-(width * (width + 1) // 2 + width + 1) // 16) * 16


def state_rows(heads, width):
    return heads * feature_rows(width) + 16


def nt(a, b):
    return lax.dot_general(a, b, (((1,), (1,)), ((), ())), preferred_element_type=F32)


def nn(a, b):
    return jnp.dot(a, b, preferred_element_type=F32)


def phi_rows(x, query):
    width, tokens = x.shape
    half = width // 2
    scale = 0.5**0.5 * width ** (-0.5)
    twice = jnp.concatenate([x, x], 0)
    rows = []
    for d in range(half):
        prod = ((x * twice[d : d + width]) * scale).astype(BF)
        if query and d:
            prod = prod * 2
        rows.append(prod)
    rows.append((x * width ** (-0.25)).astype(BF))
    cross = (x[:half] * x[half:]) * scale
    if query:
        cross = cross * 2
    pad = feature_rows(width) - (half * width + width + half)
    last = lax.broadcasted_iota(jnp.int32, (pad, tokens), 0)
    const = jnp.where(last == 0, 1.0, 0.0)
    rows.append(jnp.concatenate([cross, const], 0).astype(BF))
    return jnp.concatenate(rows, 0)


def with_ones(v):
    return jnp.concatenate([v, jnp.ones_like(v)], 1)


def lanes_of(h, count=1):
    return pl.ds(pl.multiple_of(h * HEAD_DIM, HEAD_DIM), count * HEAD_DIM)


def causal_masks():
    row = lax.broadcasted_iota(jnp.int32, (TILE, TILE), 0)
    col = lax.broadcasted_iota(jnp.int32, (TILE, TILE), 1)
    return col <= row, col > row


def prepare_kernel(kf_hbm, q_hbm, k_hbm, v_hbm, kp_ref, vp_ref, qb_ref, own_ref, before_ref, kf_ref, v_ref, sems, *, heads, width):
    feats = feature_rows(width)
    base = heads * feats
    tokens = v_ref.shape[0]
    ahead = heads // 2 * HEAD_DIM
    tail = pl.ds(tokens - WINDOW, WINDOW)
    fetch = pltpu.make_async_copy(kf_hbm, kf_ref, sems.at[3])
    fetch.start()
    whole = pltpu.make_async_copy(v_hbm, v_ref, sems.at[4])
    whole.start()
    copies = [
        pltpu.make_async_copy(k_hbm.at[tail, :ahead], kp_ref, sems.at[0]),
        pltpu.make_async_copy(v_hbm.at[tail, :ahead], vp_ref, sems.at[1]),
        pltpu.make_async_copy(q_hbm.at[:WINDOW, ahead:], qb_ref, sems.at[2]),
    ]
    for copy in copies:
        copy.start()
    fetch.wait()
    phis = [phi_rows(kf_ref[h * width : (h + 1) * width, :].astype(F32), False) for h in range(heads)]
    lane = lax.broadcasted_iota(jnp.int32, (feats, HEAD_DIM), 1)
    norms = jnp.zeros((feats, HEAD_DIM), F32)
    whole.wait()
    for h in range(heads):
        total = None
        for t in range(tokens // TILE):
            at = slice(t * TILE, (t + 1) * TILE)
            s = nn(phis[h][:, at], with_ones(v_ref[at, h * HEAD_DIM : (h + 1) * HEAD_DIM]))
            total = s if t == 0 else total + s
            if t < tokens // TILE - 1:
                before_ref[t, h * feats : (h + 1) * feats, :] = total
        own_ref[h * feats : (h + 1) * feats, :] = total[:, :HEAD_DIM].astype(BF)
        norms = jnp.where(lane == h, total[:, HEAD_DIM:], norms)
    norms = jnp.concatenate([norms, jnp.zeros((2 * HEAD_DIM - feats, HEAD_DIM), F32)], 0).T[:8]
    own_ref[base:, :] = jnp.concatenate([norms[:, :HEAD_DIM], norms[:, HEAD_DIM:]], 0).astype(BF)
    for copy in copies:
        copy.wait()
    top = kp_ref[:16, :]
    row = lax.broadcasted_iota(jnp.int32, top.shape, 0)
    kp_ref[:16, :] = jnp.where(row == 0, jnp.ones((), BF), top)


def softmax_parts(jobs, ahead=2):
    scores = []
    for i in range(len(jobs)):
        while len(scores) < min(len(jobs), i + 1 + ahead):
            query, key = jobs[len(scores)][:2]
            scores.append(nt(query(), key()))
        _, _, value, first, last, use = jobs[i]
        s, scores[i] = scores[i], None
        parts = [s[:, at : at + TILE] for at in range(0, s.shape[1], TILE)]
        if first is not None:
            parts[0] = jnp.where(first, parts[0], NEG)
        if last is not None:
            parts[-1] = jnp.where(last, parts[-1], NEG)
        top = jnp.max(functools.reduce(jnp.maximum, parts), 1, keepdims=True)
        p = jnp.concatenate([jnp.exp2((part - top) * SCALE).astype(BF) for part in parts], 1)
        acc = nn(p, with_ones(value()))
        use(top, acc[:, :HEAD_DIM], acc[:, HEAD_DIM:])


def local_kernel(q_ref, k_ref, v_ref, qf_ref, kf_ref, num_ref, den_ref, win_ref, sum_ref, top_ref, phi_ref, *, start_head, width):
    causal, beyond = causal_masks()
    tokens = q_ref.shape[0]
    feats = feature_rows(width)

    jobs = []

    def job(g, start):
        h = g + start_head
        at = slice(start, start + TILE)
        keys = slice(max(0, start - WINDOW), start + TILE)
        lanes = slice(g * HEAD_DIM, (g + 1) * HEAD_DIM)
        wide = slice(h * HEAD_DIM, (h + 1) * HEAD_DIM)

        def use(top, out, total):
            win_ref[at, lanes] = out
            sum_ref[at, lanes] = total
            if start < WINDOW:
                top_ref[at, lanes] = jnp.broadcast_to(top, (TILE, HEAD_DIM))
            r = nn(phi_ref[g, at, HEAD_DIM:], kfs[g][:, at])
            part = width ** (-0.25)
            t = jnp.where(causal, (r * (0.5 * part * part) + part) * r + 1.0, 0.0)
            both = nn(t.astype(BF), with_ones(v_ref[at, wide]))
            num_ref[at, lanes] = both[:, :HEAD_DIM]
            den_ref[at, lanes] = both[:, HEAD_DIM:]

        first = beyond if start >= WINDOW else None
        jobs.append((lambda: q_ref[at, wide], lambda: k_ref[keys, wide], lambda: v_ref[keys, wide], first, causal, use))

    kfs = []
    for g in range(num_ref.shape[1] // HEAD_DIM):
        h = g + start_head
        rows = slice(h * width, (h + 1) * width)
        phi_ref[g] = phi_rows(qf_ref[rows, :].astype(F32), True).astype(F32).T.astype(BF)
        kfs.append(jnp.concatenate([kf_ref[rows, :], jnp.zeros((feats - HEAD_DIM - width, tokens), BF)], 0))
        for start in range(0, tokens, TILE):
            job(g, start)
    softmax_parts(jobs)


def serve_kernel(qb_ref, k_ref, v_ref, out_ref, *, behind):
    _, beyond = causal_masks()
    base = k_ref.shape[0] - WINDOW
    count = qb_ref.shape[1] // HEAD_DIM
    lane = lax.broadcasted_iota(jnp.int32, (TILE, HEAD_DIM), 1)
    jobs = []
    stats = [jnp.zeros((TILE, HEAD_DIM), F32) for _ in range(WINDOW // TILE)]

    def job(start, g):
        at = slice(start, start + TILE)
        keys = slice(base + start, base + WINDOW)
        lanes = slice(g * HEAD_DIM, (g + 1) * HEAD_DIM)
        wide = slice((behind + g) * HEAD_DIM, (behind + g + 1) * HEAD_DIM)

        def use(top, out, total):
            out_ref[at, lanes] = out.astype(BF)
            stat = jnp.where(lane == g, top, stats[start // TILE])
            stats[start // TILE] = jnp.where(lane == count + g, total, stat)

        jobs.append((lambda: qb_ref[at, lanes], lambda: k_ref[keys, wide], lambda: v_ref[keys, wide], beyond, None, use))

    for start in range(0, WINDOW, TILE):
        for g in range(count):
            job(start, g)
    softmax_parts(jobs)
    for i, stat in enumerate(stats):
        stat = stat.T[: 2 * count]
        high = stat.astype(BF).astype(F32)
        middle = (stat - high).astype(BF).astype(F32)
        low = stat - high - middle
        pad = jnp.ones((16 - 6 * count, TILE), F32)
        rows = jnp.concatenate([high, middle, low, pad], 0)
        out_ref[WINDOW + 16 * i : WINDOW + 16 * (i + 1), :] = rows.astype(BF)


def merged(window, mine, total, top, out, count, later):
    top = jnp.where(later, top, 2 * NEG)
    most = jnp.maximum(mine, top)
    here = jnp.exp2((mine - most) * SCALE)
    there = jnp.exp2((top - most) * SCALE)
    return window * here + out * there, total * here + count * there


def power_of(mixed):
    return jnp.mean(mixed * mixed, 1, keepdims=True) + 1e-05


def normed(mixed, power, gain):
    return (mixed * lax.rsqrt(power) * gain).astype(BF)


def halo_jobs(q_ref, kp_ref, vp_ref, win_ref, sum_ref, top_ref, near_ref, both_ref):
    _, beyond = causal_masks()
    later = kp_ref[:1, :1].astype(F32) > 0
    jobs = []

    def job(g, start):
        at = slice(start, start + TILE)
        keys = slice(start, WINDOW)
        cols = slice(g * HEAD_DIM, (g + 1) * HEAD_DIM)

        def use(top, out, total):
            near_ref[at, cols], both_ref[at, cols] = merged(
                win_ref[at, cols], top_ref[at, cols], sum_ref[at, cols], top, out, total, later
            )

        jobs.append((lambda: q_ref[at, cols], lambda: kp_ref[keys, cols], lambda: vp_ref[keys, cols], beyond, None, use))

    for g in range(kp_ref.shape[1] // HEAD_DIM):
        for start in range(0, WINDOW, TILE):
            job(g, start)
    return jobs


def first_final_kernel(q_ref, kp_ref, vp_ref, top_ref, *refs, heads, width):
    halves = [refs[:5], refs[5:10]]
    *prior_refs, before_ref, gain_hbm, out_hbm, lin_ref, gain_b_ref, gain_ref, near_ref, both_ref, out_ref, sems = refs[10:]
    count = heads // 2
    tokens = halves[0][0].shape[0]
    feats = feature_rows(width)
    base = heads * feats
    fetch = pltpu.make_async_copy(gain_hbm, gain_ref, sems.at[heads])
    fetch.start()

    def prior(rows):
        return functools.reduce(jnp.add, [ref[rows, :].astype(F32) for ref in prior_refs])

    tail = jnp.concatenate([prior(slice(base, base + 16)), jnp.zeros((HEAD_DIM - 16, HEAD_DIM), F32)], 0).T

    def state(h):
        norm = [
            jnp.broadcast_to(tail[:, h : h + 1], (HEAD_DIM, HEAD_DIM)),
            jnp.broadcast_to(tail[: feats - HEAD_DIM, 8 + h : 9 + h], (feats - HEAD_DIM, HEAD_DIM)),
        ]
        return jnp.concatenate([prior(slice(h * feats, (h + 1) * feats)), jnp.concatenate(norm, 0)], 1)

    softmax_parts(halo_jobs(q_ref, kp_ref, vp_ref, halves[0][2], halves[0][3], top_ref, near_ref, both_ref))
    order = [(h, start) for h in list(range(count, heads)) + list(range(count)) for start in range(0, tokens, TILE)]
    states, lins, copies = {}, [], []
    for i, (h, start) in enumerate(order):
        while len(lins) < min(len(order), i + 3):
            hn, sn = order[len(lins)]
            rows = slice(hn * feats, (hn + 1) * feats)
            if hn not in states:
                states[hn] = state(hn)
            both = states[hn] if sn == 0 else states[hn] + before_ref[sn // TILE - 1, rows, :]
            lins.append(nn(halves[hn // count][4][hn % count, sn : sn + TILE, :], both.astype(BF)))
        lin, lins[i] = lins[i], None
        part, g = h // count, h % count
        num_ref, den_ref, win_ref, sum_ref = halves[part][:4]
        at = slice(start, start + TILE)
        cols = slice(g * HEAD_DIM, (g + 1) * HEAD_DIM)
        wide = slice(h * HEAD_DIM, (h + 1) * HEAD_DIM)
        num = num_ref[at, cols] + lin[:, :HEAD_DIM]
        den = den_ref[at, cols] + lin[:, HEAD_DIM:]
        if start < WINDOW and part == 1:
            lin_ref[at, cols] = num / den
        else:
            if not copies and start == WINDOW:
                fetch.wait()
                gain_b_ref[...] = gain_ref[:, count * HEAD_DIM :]
            if start < WINDOW:
                window, total = near_ref[at, cols], both_ref[at, cols]
            else:
                window, total = win_ref[at, cols], sum_ref[at, cols]
            mixed = num / den + window / total
            out_ref[at, wide] = normed(mixed, power_of(mixed), gain_ref[:, wide])
        if start + TILE == tokens:
            area = (pl.ds(WINDOW * part, tokens - WINDOW * part), pl.ds(h * HEAD_DIM, HEAD_DIM))
            copies.append(pltpu.make_async_copy(out_ref.at[area], out_hbm.at[area], sems.at[h]))
            copies[-1].start()
    for copy in copies:
        copy.wait()


def last_final_kernel(ob_ref, lin_ref, win_ref, sum_ref, top_ref, gain_ref, _, out_hbm, out_ref, sems):
    count = lin_ref.shape[1] // HEAD_DIM
    ahead = out_hbm.shape[1] - count * HEAD_DIM
    later = ob_ref[WINDOW + 15 : WINDOW + 16, :1].astype(F32) > 0
    stats = []
    n = 2 * count
    for i in range(WINDOW // TILE):
        got = ob_ref[WINDOW + 16 * i : WINDOW + 16 * (i + 1), :].astype(F32)
        stats.append(got[:n] + got[n : 2 * n] + got[2 * n : 3 * n])
    stats.append(jnp.zeros((HEAD_DIM - n * len(stats), TILE), F32))
    stats = jnp.concatenate(stats, 0).T
    parts = [(start, g) for start in range(0, WINDOW, TILE) for g in range(count)]

    def place(start, g):
        return slice(start, start + TILE), slice(g * HEAD_DIM, (g + 1) * HEAD_DIM)

    def stat(start, lane):
        lane += start // TILE * n
        return stats[:, lane : lane + 1]

    windows = []
    for start, g in parts:
        at = place(start, g)
        windows.append(merged(win_ref[at], top_ref[at], sum_ref[at], stat(start, g), ob_ref[at].astype(F32), stat(start, count + g), later))
    mixed = [lin_ref[place(*part)] + window / total for part, (window, total) in zip(parts, windows)]
    powers = [power_of(m) for m in mixed]
    for part, m, power in zip(parts, mixed, powers):
        at = place(*part)
        out_ref[at] = normed(m, power, gain_ref[:, at[1]])
    copy = pltpu.make_async_copy(out_ref, out_hbm.at[:WINDOW, ahead:], sems.at[0])
    copy.start()
    copy.wait()


def relay_kernel(own_ref, got_ref, _, sum_ref, pass_ref):
    sum_ref[...] = own_ref[...] + got_ref[...]


def shifted(value, axis, steps):
    count = lax.axis_size(axis)
    pairs = [(i, i + steps) for i in range(count) if 0 <= i + steps < count]
    return lax.ppermute(value, axis, pairs)


def body(q_feat, k_feat, swa_query, swa_key, values, gain):
    tokens, columns = swa_query.shape
    heads = columns // HEAD_DIM
    half = heads // 2
    width = q_feat.shape[1] // heads
    feats = feature_rows(width)
    rows = state_rows(heads, width)
    count = lax.axis_size("seq")
    vmem = pl.BlockSpec(memory_space=pltpu.VMEM)
    hbm = pl.BlockSpec(memory_space=pltpu.HBM)
    grant = pltpu.CompilerParams(vmem_limit_bytes=GRANT)
    qft, kft = q_feat.T, k_feat.T

    in_hbm = lambda *arrays: [pltpu.with_memory_space_constraint(a, pltpu.HBM) for a in arrays]
    kp, vp, qb, own, before = pl.pallas_call(
        functools.partial(prepare_kernel, heads=heads, width=width),
        out_shape=(
            jax.ShapeDtypeStruct((WINDOW, half * HEAD_DIM), BF),
            jax.ShapeDtypeStruct((WINDOW, half * HEAD_DIM), BF),
            jax.ShapeDtypeStruct((WINDOW, half * HEAD_DIM), BF),
            jax.ShapeDtypeStruct((rows, HEAD_DIM), BF),
            jax.ShapeDtypeStruct((tokens // TILE - 1, heads * feats, 2 * HEAD_DIM), F32),
        ),
        in_specs=[hbm] * 4,
        out_specs=(vmem,) * 5,
        scratch_shapes=[
            pltpu.VMEM(kft.shape, BF),
            pltpu.VMEM((tokens, columns), BF),
            pltpu.SemaphoreType.DMA((5,)),
        ],
        compiler_params=grant,
        cost_estimate=pl.CostEstimate(flops=1 << 30, bytes_accessed=3 << 20, transcendentals=0),
        name="prepare",
    )(*in_hbm(kft, swa_query, swa_key, values))

    def local(start_head, flops):
        wide = jax.ShapeDtypeStruct((tokens, half * HEAD_DIM), F32)
        near = jax.ShapeDtypeStruct((WINDOW, half * HEAD_DIM), F32)
        return pl.pallas_call(
            functools.partial(local_kernel, start_head=start_head, width=width),
            out_shape=(wide, wide, wide, wide, near, jax.ShapeDtypeStruct((half, tokens, feats), BF)),
            in_specs=[vmem] * 5,
            out_specs=(vmem,) * 6,
            compiler_params=grant,
            cost_estimate=pl.CostEstimate(flops=flops, bytes_accessed=1 << 20, transcendentals=1 << 10),
            name="local",
        )(swa_query, swa_key, values, qft, kft)

    if count <= 4:
        running, prior = own, []
        for i in range(count - 1):
            got = lax.ppermute(running, "seq", [(i, i + 1)])
            prior.append(got)
            running = own + got
            if i == 0:
                asked = shifted(qb, "seq", -1)
                running, vp = pl.pallas_call(
                    relay_kernel,
                    out_shape=(jax.ShapeDtypeStruct(own.shape, BF), jax.ShapeDtypeStruct(vp.shape, BF)),
                    in_specs=[vmem] * 3,
                    out_specs=(vmem,) * 2,
                    input_output_aliases={2: 1},
                    compiler_params=grant,
                    cost_estimate=pl.CostEstimate(flops=RL, bytes_accessed=1 << 19, transcendentals=0),
                    name="relay",
                )(own, got, vp)
                halo = shifted(kp, "seq", 1), shifted(vp, "seq", 1)
    else:
        running, prior, distance = own, [], 1
        halo = shifted(kp, "seq", 1), shifted(vp, "seq", 1)
        asked = shifted(qb, "seq", -1)
        while distance < count:
            got = shifted(running, "seq", distance)
            prior.append(got)
            running = running + got
            distance *= 2

    local_a = local(0, LA)
    answer = pl.pallas_call(
        functools.partial(serve_kernel, behind=half),
        out_shape=jax.ShapeDtypeStruct((WINDOW + 16 * (WINDOW // TILE), half * HEAD_DIM), BF),
        in_specs=[vmem] * 3,
        out_specs=vmem,
        compiler_params=grant,
        cost_estimate=pl.CostEstimate(flops=SV, bytes_accessed=1 << 20, transcendentals=1 << 10),
        name="serve",
    )(asked, swa_key, values)
    answered = shifted(answer, "seq", 1)
    local_b = local(half, LB)

    num_a, den_a, win_a, sum_a, top_a, phi_a = local_a
    num_b, den_b, win_b, sum_b, top_b, phi_b = local_b
    gain_row = in_hbm(gain.reshape(1, columns))
    near = jax.ShapeDtypeStruct((WINDOW, half * HEAD_DIM), F32)
    operands = (swa_query, *halo, top_a, num_a, den_a, win_a, sum_a, phi_a, num_b, den_b, win_b, sum_b, phi_b, *prior, before)
    out, lin, gain_b = pl.pallas_call(
        functools.partial(first_final_kernel, heads=heads, width=width),
        out_shape=(
            jax.ShapeDtypeStruct((tokens, columns), BF),
            near,
            jax.ShapeDtypeStruct((1, half * HEAD_DIM), F32),
        ),
        in_specs=[vmem] * len(operands) + [hbm],
        out_specs=(hbm, vmem, vmem),
        scratch_shapes=[
            pltpu.VMEM((1, columns), F32),
            pltpu.VMEM(near.shape, F32),
            pltpu.VMEM(near.shape, F32),
            pltpu.VMEM((tokens, columns), BF),
            pltpu.SemaphoreType.DMA((heads + 1,)),
        ],
        compiler_params=grant,
        cost_estimate=pl.CostEstimate(flops=FN, bytes_accessed=12 << 20, transcendentals=1 << 20),
        name="final",
    )(*operands, *gain_row)
    return pl.pallas_call(
        last_final_kernel,
        out_shape=jax.ShapeDtypeStruct((tokens, columns), BF),
        in_specs=[vmem] * 6 + [hbm],
        out_specs=hbm,
        scratch_shapes=[
            pltpu.VMEM((WINDOW, half * HEAD_DIM), BF),
            pltpu.SemaphoreType.DMA((1,)),
        ],
        input_output_aliases={6: 0},
        compiler_params=grant,
        cost_estimate=pl.CostEstimate(flops=1 << 20, bytes_accessed=3 << 20, transcendentals=1 << 19),
        name="last",
    )(answered, lin, win_b, sum_b, top_b, gain_b, out)


def solution(mesh):
    tokens = P(("groups", "seq"), "head")
    return jax.shard_map(
        body, mesh=mesh, in_specs=(tokens,) * 5 + (P("head"),), out_specs=tokens, check_vma=False
    )
```

```python
import functools

import jax
import jax.numpy as jnp
from jax import lax
from jax.experimental import pallas as pl
from jax.experimental.pallas import tpu as pltpu
from jax.sharding import PartitionSpec as P

HEAD_DIM = 128
WINDOW = 512
TILE = 256
NEG = -1e30
SCALE = HEAD_DIM ** (-0.5) * 1.4426950408889634
BF = jnp.bfloat16
F32 = jnp.float32
GRANT = 16 << 20
LA = 4194304000
LB = 1048576000
SV = 314572800
PR = 1 << 30
RL = 104857
FN = 2097152000


def feature_rows(width):
    return -(-(width * (width + 1) // 2 + width + 1) // 16) * 16


def state_rows(heads, width):
    return heads * feature_rows(width) + 16


def nt(a, b):
    return lax.dot_general(a, b, (((1,), (1,)), ((), ())), preferred_element_type=F32)


def nn(a, b):
    return jnp.dot(a, b, preferred_element_type=F32)


def phi_rows(x, query):
    width, tokens = x.shape
    half = width // 2
    scale = 0.5**0.5 * width ** (-0.5)
    twice = jnp.concatenate([x, x], 0)
    rows = []
    for d in range(half):
        prod = ((x * twice[d : d + width]) * scale).astype(BF)
        if query and d:
            prod = prod * 2
        rows.append(prod)
    rows.append((x * width ** (-0.25)).astype(BF))
    cross = (x[:half] * x[half:]) * scale
    if query:
        cross = cross * 2
    pad = feature_rows(width) - (half * width + width + half)
    last = lax.broadcasted_iota(jnp.int32, (pad, tokens), 0)
    const = jnp.where(last == 0, 1.0, 0.0)
    rows.append(jnp.concatenate([cross, const], 0).astype(BF))
    return jnp.concatenate(rows, 0)


def with_ones(v):
    return jnp.concatenate([v, jnp.ones_like(v)], 1)


def lanes_of(h, count=1):
    return pl.ds(pl.multiple_of(h * HEAD_DIM, HEAD_DIM), count * HEAD_DIM)


def causal_masks():
    row = lax.broadcasted_iota(jnp.int32, (TILE, TILE), 0)
    col = lax.broadcasted_iota(jnp.int32, (TILE, TILE), 1)
    return col <= row, col > row


def prepare_kernel(kf_hbm, q_hbm, k_hbm, v_hbm, kp_ref, vp_ref, qb_ref, own_ref, before_ref, kf_ref, v_ref, sems, *, heads, width):
    feats = feature_rows(width)
    base = heads * feats
    tokens = v_ref.shape[0]
    ahead = heads // 2 * HEAD_DIM
    tail = pl.ds(tokens - WINDOW, WINDOW)
    fetch = pltpu.make_async_copy(kf_hbm, kf_ref, sems.at[3])
    fetch.start()
    whole = pltpu.make_async_copy(v_hbm, v_ref, sems.at[4])
    whole.start()
    copies = [
        pltpu.make_async_copy(k_hbm.at[tail, :ahead], kp_ref, sems.at[0]),
        pltpu.make_async_copy(v_hbm.at[tail, :ahead], vp_ref, sems.at[1]),
        pltpu.make_async_copy(q_hbm.at[:WINDOW, ahead:], qb_ref, sems.at[2]),
    ]
    for copy in copies:
        copy.start()
    fetch.wait()
    phis = [phi_rows(kf_ref[h * width : (h + 1) * width, :].astype(F32), False) for h in range(heads)]
    lane = lax.broadcasted_iota(jnp.int32, (feats, HEAD_DIM), 1)
    norms = jnp.zeros((feats, HEAD_DIM), F32)
    whole.wait()
    for h in range(heads):
        total = None
        for t in range(tokens // TILE):
            at = slice(t * TILE, (t + 1) * TILE)
            s = nn(phis[h][:, at], with_ones(v_ref[at, h * HEAD_DIM : (h + 1) * HEAD_DIM]))
            total = s if t == 0 else total + s
            if t < tokens // TILE - 1:
                before_ref[t, h * feats : (h + 1) * feats, :] = total
        own_ref[h * feats : (h + 1) * feats, :] = total[:, :HEAD_DIM].astype(BF)
        norms = jnp.where(lane == h, total[:, HEAD_DIM:], norms)
    norms = jnp.concatenate([norms, jnp.zeros((2 * HEAD_DIM - feats, HEAD_DIM), F32)], 0).T[:8]
    own_ref[base:, :] = jnp.concatenate([norms[:, :HEAD_DIM], norms[:, HEAD_DIM:]], 0).astype(BF)
    for copy in copies:
        copy.wait()
    top = kp_ref[:16, :]
    row = lax.broadcasted_iota(jnp.int32, top.shape, 0)
    kp_ref[:16, :] = jnp.where(row == 0, jnp.ones((), BF), top)


def softmax_parts(jobs, ahead=2):
    scores = []
    for i in range(len(jobs)):
        while len(scores) < min(len(jobs), i + 1 + ahead):
            query, key = jobs[len(scores)][:2]
            scores.append(nt(query(), key()))
        _, _, value, first, last, use = jobs[i]
        s, scores[i] = scores[i], None
        parts = [s[:, at : at + TILE] for at in range(0, s.shape[1], TILE)]
        if first is not None:
            parts[0] = jnp.where(first, parts[0], NEG)
        if last is not None:
            parts[-1] = jnp.where(last, parts[-1], NEG)
        top = jnp.max(functools.reduce(jnp.maximum, parts), 1, keepdims=True)
        p = jnp.concatenate([jnp.exp2((part - top) * SCALE).astype(BF) for part in parts], 1)
        acc = nn(p, with_ones(value()))
        use(top, acc[:, :HEAD_DIM], acc[:, HEAD_DIM:])


def local_kernel(q_ref, k_ref, v_ref, qf_ref, kf_ref, num_ref, den_ref, win_ref, sum_ref, top_ref, phi_ref, *, start_head, width):
    causal, beyond = causal_masks()
    tokens = q_ref.shape[0]
    feats = feature_rows(width)

    jobs = []

    def job(g, start):
        h = g + start_head
        at = slice(start, start + TILE)
        keys = slice(max(0, start - WINDOW), start + TILE)
        lanes = slice(g * HEAD_DIM, (g + 1) * HEAD_DIM)
        wide = slice(h * HEAD_DIM, (h + 1) * HEAD_DIM)

        def use(top, out, total):
            win_ref[at, lanes] = out
            sum_ref[at, lanes] = total
            if start < WINDOW:
                top_ref[at, lanes] = jnp.broadcast_to(top, (TILE, HEAD_DIM))
            r = nn(phi_ref[g, at, HEAD_DIM:], kfs[g][:, at])
            part = width ** (-0.25)
            t = jnp.where(causal, (r * (0.5 * part * part) + part) * r + 1.0, 0.0)
            both = nn(t.astype(BF), with_ones(v_ref[at, wide]))
            num_ref[at, lanes] = both[:, :HEAD_DIM]
            den_ref[at, lanes] = both[:, HEAD_DIM:]

        first = beyond if start >= WINDOW else None
        jobs.append((lambda: q_ref[at, wide], lambda: k_ref[keys, wide], lambda: v_ref[keys, wide], first, causal, use))

    kfs = []
    for g in range(num_ref.shape[1] // HEAD_DIM):
        h = g + start_head
        rows = slice(h * width, (h + 1) * width)
        phi_ref[g] = phi_rows(qf_ref[rows, :].astype(F32), True).astype(F32).T.astype(BF)
        kfs.append(jnp.concatenate([kf_ref[rows, :], jnp.zeros((feats - HEAD_DIM - width, tokens), BF)], 0))
        for start in range(0, tokens, TILE):
            job(g, start)
    softmax_parts(jobs)


def serve_kernel(_, qb_ref, k_ref, v_ref, __, out_ref, *, behind):
    _, beyond = causal_masks()
    base = k_ref.shape[0] - WINDOW
    count = qb_ref.shape[1] // HEAD_DIM
    lane = lax.broadcasted_iota(jnp.int32, (TILE, HEAD_DIM), 1)
    jobs = []
    stats = [jnp.zeros((TILE, HEAD_DIM), F32) for _ in range(WINDOW // TILE)]

    def job(start, g):
        at = slice(start, start + TILE)
        keys = slice(base + start, base + WINDOW)
        lanes = slice(g * HEAD_DIM, (g + 1) * HEAD_DIM)
        wide = slice((behind + g) * HEAD_DIM, (behind + g + 1) * HEAD_DIM)

        def use(top, out, total):
            out_ref[at, lanes] = out.astype(BF)
            stat = jnp.where(lane == g, top, stats[start // TILE])
            stats[start // TILE] = jnp.where(lane == count + g, total, stat)

        jobs.append((lambda: qb_ref[at, lanes], lambda: k_ref[keys, wide], lambda: v_ref[keys, wide], beyond, None, use))

    for start in range(0, WINDOW, TILE):
        for g in range(count):
            job(start, g)
    softmax_parts(jobs)
    for i, stat in enumerate(stats):
        stat = stat.T[: 2 * count]
        high = stat.astype(BF).astype(F32)
        middle = (stat - high).astype(BF).astype(F32)
        low = stat - high - middle
        pad = jnp.ones((16 - 6 * count, TILE), F32)
        rows = jnp.concatenate([high, middle, low, pad], 0)
        out_ref[WINDOW + 16 * i : WINDOW + 16 * (i + 1), :] = rows.astype(BF)


def merged(window, mine, total, top, out, count, later):
    top = jnp.where(later, top, 2 * NEG)
    most = jnp.maximum(mine, top)
    here = jnp.exp2((mine - most) * SCALE)
    there = jnp.exp2((top - most) * SCALE)
    return window * here + out * there, total * here + count * there


def power_of(mixed):
    return jnp.mean(mixed * mixed, 1, keepdims=True) + 1e-05


def normed(mixed, power, gain):
    return (mixed * lax.rsqrt(power) * gain).astype(BF)


def halo_jobs(q_ref, kp_ref, vp_ref, win_ref, sum_ref, top_ref, near_ref, both_ref):
    _, beyond = causal_masks()
    later = kp_ref[:1, :1].astype(F32) > 0
    jobs = []

    def job(g, start):
        at = slice(start, start + TILE)
        keys = slice(start, WINDOW)
        cols = slice(g * HEAD_DIM, (g + 1) * HEAD_DIM)

        def use(top, out, total):
            near_ref[at, cols], both_ref[at, cols] = merged(
                win_ref[at, cols], top_ref[at, cols], sum_ref[at, cols], top, out, total, later
            )

        jobs.append((lambda: q_ref[at, cols], lambda: kp_ref[keys, cols], lambda: vp_ref[keys, cols], beyond, None, use))

    for g in range(kp_ref.shape[1] // HEAD_DIM):
        for start in range(0, WINDOW, TILE):
            job(g, start)
    return jobs


def first_final_kernel(q_ref, kp_ref, vp_ref, top_ref, *refs, heads, width):
    halves = [refs[:5], refs[5:10]]
    *prior_refs, before_ref, gain_hbm, out_hbm, lin_ref, gain_b_ref, gain_ref, near_ref, both_ref, out_ref, sems = refs[10:]
    count = heads // 2
    tokens = halves[0][0].shape[0]
    feats = feature_rows(width)
    base = heads * feats
    fetch = pltpu.make_async_copy(gain_hbm, gain_ref, sems.at[heads])
    fetch.start()

    def prior(rows):
        return functools.reduce(jnp.add, [ref[rows, :].astype(F32) for ref in prior_refs])

    tail = jnp.concatenate([prior(slice(base, base + 16)), jnp.zeros((HEAD_DIM - 16, HEAD_DIM), F32)], 0).T

    def state(h):
        norm = [
            jnp.broadcast_to(tail[:, h : h + 1], (HEAD_DIM, HEAD_DIM)),
            jnp.broadcast_to(tail[: feats - HEAD_DIM, 8 + h : 9 + h], (feats - HEAD_DIM, HEAD_DIM)),
        ]
        return jnp.concatenate([prior(slice(h * feats, (h + 1) * feats)), jnp.concatenate(norm, 0)], 1)

    softmax_parts(halo_jobs(q_ref, kp_ref, vp_ref, halves[0][2], halves[0][3], top_ref, near_ref, both_ref))
    order = [(h, start) for h in list(range(count, heads)) + list(range(count)) for start in range(0, tokens, TILE)]
    states, lins, copies = {}, [], []
    for i, (h, start) in enumerate(order):
        while len(lins) < min(len(order), i + 3):
            hn, sn = order[len(lins)]
            rows = slice(hn * feats, (hn + 1) * feats)
            if hn not in states:
                states[hn] = state(hn)
            both = states[hn] if sn == 0 else states[hn] + before_ref[sn // TILE - 1, rows, :]
            lins.append(nn(halves[hn // count][4][hn % count, sn : sn + TILE, :], both.astype(BF)))
        lin, lins[i] = lins[i], None
        part, g = h // count, h % count
        num_ref, den_ref, win_ref, sum_ref = halves[part][:4]
        at = slice(start, start + TILE)
        cols = slice(g * HEAD_DIM, (g + 1) * HEAD_DIM)
        wide = slice(h * HEAD_DIM, (h + 1) * HEAD_DIM)
        num = num_ref[at, cols] + lin[:, :HEAD_DIM]
        den = den_ref[at, cols] + lin[:, HEAD_DIM:]
        if start < WINDOW and part == 1:
            lin_ref[at, cols] = num / den
        else:
            if not copies and start == WINDOW:
                fetch.wait()
                gain_b_ref[...] = gain_ref[:, count * HEAD_DIM :]
            if start < WINDOW:
                window, total = near_ref[at, cols], both_ref[at, cols]
            else:
                window, total = win_ref[at, cols], sum_ref[at, cols]
            mixed = num / den + window / total
            out_ref[at, wide] = normed(mixed, power_of(mixed), gain_ref[:, wide])
        if start + TILE == tokens:
            area = (pl.ds(WINDOW * part, tokens - WINDOW * part), pl.ds(h * HEAD_DIM, HEAD_DIM))
            copies.append(pltpu.make_async_copy(out_ref.at[area], out_hbm.at[area], sems.at[h]))
            copies[-1].start()
    for copy in copies:
        copy.wait()


def last_final_kernel(ob_ref, lin_ref, win_ref, sum_ref, top_ref, gain_ref, _, out_hbm, out_ref, sems):
    count = lin_ref.shape[1] // HEAD_DIM
    ahead = out_hbm.shape[1] - count * HEAD_DIM
    later = ob_ref[WINDOW + 15 : WINDOW + 16, :1].astype(F32) > 0
    stats = []
    n = 2 * count
    for i in range(WINDOW // TILE):
        got = ob_ref[WINDOW + 16 * i : WINDOW + 16 * (i + 1), :].astype(F32)
        stats.append(got[:n] + got[n : 2 * n] + got[2 * n : 3 * n])
    stats.append(jnp.zeros((HEAD_DIM - n * len(stats), TILE), F32))
    stats = jnp.concatenate(stats, 0).T
    parts = [(start, g) for start in range(0, WINDOW, TILE) for g in range(count)]

    def place(start, g):
        return slice(start, start + TILE), slice(g * HEAD_DIM, (g + 1) * HEAD_DIM)

    def stat(start, lane):
        lane += start // TILE * n
        return stats[:, lane : lane + 1]

    windows = []
    for start, g in parts:
        at = place(start, g)
        windows.append(merged(win_ref[at], top_ref[at], sum_ref[at], stat(start, g), ob_ref[at].astype(F32), stat(start, count + g), later))
    mixed = [lin_ref[place(*part)] + window / total for part, (window, total) in zip(parts, windows)]
    powers = [power_of(m) for m in mixed]
    for part, m, power in zip(parts, mixed, powers):
        at = place(*part)
        out_ref[at] = normed(m, power, gain_ref[:, at[1]])
    copy = pltpu.make_async_copy(out_ref, out_hbm.at[:WINDOW, ahead:], sems.at[0])
    copy.start()
    copy.wait()


def relay_kernel(own_ref, got_ref, _, sum_ref, pass_ref):
    sum_ref[...] = own_ref[...] + got_ref[...]


def shifted(value, axis, steps):
    count = lax.axis_size(axis)
    pairs = [(i, i + steps) for i in range(count) if 0 <= i + steps < count]
    return lax.ppermute(value, axis, pairs)


def body(q_feat, k_feat, swa_query, swa_key, values, gain):
    tokens, columns = swa_query.shape
    heads = columns // HEAD_DIM
    half = heads // 2
    width = q_feat.shape[1] // heads
    feats = feature_rows(width)
    rows = state_rows(heads, width)
    count = lax.axis_size("seq")
    vmem = pl.BlockSpec(memory_space=pltpu.VMEM)
    hbm = pl.BlockSpec(memory_space=pltpu.HBM)
    grant = pltpu.CompilerParams(vmem_limit_bytes=GRANT)
    qft, kft = q_feat.T, k_feat.T

    in_hbm = lambda *arrays: [pltpu.with_memory_space_constraint(a, pltpu.HBM) for a in arrays]
    kp, vp, qb, own, before = pl.pallas_call(
        functools.partial(prepare_kernel, heads=heads, width=width),
        out_shape=(
            jax.ShapeDtypeStruct((WINDOW, half * HEAD_DIM), BF),
            jax.ShapeDtypeStruct((WINDOW, half * HEAD_DIM), BF),
            jax.ShapeDtypeStruct((WINDOW, half * HEAD_DIM), BF),
            jax.ShapeDtypeStruct((rows, HEAD_DIM), BF),
            jax.ShapeDtypeStruct((tokens // TILE - 1, heads * feats, 2 * HEAD_DIM), F32),
        ),
        in_specs=[hbm] * 4,
        out_specs=(vmem,) * 5,
        scratch_shapes=[
            pltpu.VMEM(kft.shape, BF),
            pltpu.VMEM((tokens, columns), BF),
            pltpu.SemaphoreType.DMA((5,)),
        ],
        compiler_params=grant,
        cost_estimate=pl.CostEstimate(flops=1 << 30, bytes_accessed=3 << 20, transcendentals=0),
        name="prepare",
    )(*in_hbm(kft, swa_query, swa_key, values))

    def local(start_head, flops):
        wide = jax.ShapeDtypeStruct((tokens, half * HEAD_DIM), F32)
        near = jax.ShapeDtypeStruct((WINDOW, half * HEAD_DIM), F32)
        return pl.pallas_call(
            functools.partial(local_kernel, start_head=start_head, width=width),
            out_shape=(wide, wide, wide, wide, near, jax.ShapeDtypeStruct((half, tokens, feats), BF)),
            in_specs=[vmem] * 5,
            out_specs=(vmem,) * 6,
            compiler_params=grant,
            cost_estimate=pl.CostEstimate(flops=flops, bytes_accessed=1 << 20, transcendentals=1 << 10),
            name="local",
        )(swa_query, swa_key, values, qft, kft)

    local_a = local(0, LA)

    def serve(asked):
        return pl.pallas_call(
            functools.partial(serve_kernel, behind=half),
            out_shape=jax.ShapeDtypeStruct((WINDOW + 16 * (WINDOW // TILE), half * HEAD_DIM), BF),
            in_specs=[vmem] * 5,
            out_specs=vmem,
            compiler_params=grant,
            cost_estimate=pl.CostEstimate(flops=SV, bytes_accessed=1 << 20, transcendentals=1 << 10),
            name="serve",
        )(halo[0], asked, swa_key, values, local_a[4])

    def relay(got, passed):
        return pl.pallas_call(
            relay_kernel,
            out_shape=(jax.ShapeDtypeStruct(own.shape, BF), jax.ShapeDtypeStruct(passed.shape, BF)),
            in_specs=[vmem] * 3,
            out_specs=(vmem,) * 2,
            input_output_aliases={2: 1},
            compiler_params=grant,
            cost_estimate=pl.CostEstimate(flops=RL, bytes_accessed=1 << 19, transcendentals=0),
            name="relay",
        )(own, got, passed)

    if count <= 4:
        running, prior = own, []
        for i in range(count - 1):
            got = lax.ppermute(running, "seq", [(i, i + 1)])
            prior.append(got)
            if i == 0:
                halo_key = shifted(kp, "seq", 1)
                asked = shifted(qb, "seq", -1)
                running, vp = relay(got, vp)
                halo = halo_key, shifted(vp, "seq", 1)
                answer = serve(asked)
            elif i == 1:
                running, answer = relay(got, answer)
            else:
                running = own + got
    else:
        running, prior, distance = own, [], 1
        halo = shifted(kp, "seq", 1), shifted(vp, "seq", 1)
        answer = serve(shifted(qb, "seq", -1))
        while distance < count:
            got = shifted(running, "seq", distance)
            prior.append(got)
            running = running + got
            distance *= 2

    answered = shifted(answer, "seq", 1)
    local_b = local(half, LB)

    num_a, den_a, win_a, sum_a, top_a, phi_a = local_a
    num_b, den_b, win_b, sum_b, top_b, phi_b = local_b
    gain_row = in_hbm(gain.reshape(1, columns))
    near = jax.ShapeDtypeStruct((WINDOW, half * HEAD_DIM), F32)
    operands = (swa_query, *halo, top_a, num_a, den_a, win_a, sum_a, phi_a, num_b, den_b, win_b, sum_b, phi_b, *prior, before)
    out, lin, gain_b = pl.pallas_call(
        functools.partial(first_final_kernel, heads=heads, width=width),
        out_shape=(
            jax.ShapeDtypeStruct((tokens, columns), BF),
            near,
            jax.ShapeDtypeStruct((1, half * HEAD_DIM), F32),
        ),
        in_specs=[vmem] * len(operands) + [hbm],
        out_specs=(hbm, vmem, vmem),
        scratch_shapes=[
            pltpu.VMEM((1, columns), F32),
            pltpu.VMEM(near.shape, F32),
            pltpu.VMEM(near.shape, F32),
            pltpu.VMEM((tokens, columns), BF),
            pltpu.SemaphoreType.DMA((heads + 1,)),
        ],
        compiler_params=grant,
        cost_estimate=pl.CostEstimate(flops=FN, bytes_accessed=12 << 20, transcendentals=1 << 20),
        name="final",
    )(*operands, *gain_row)
    return pl.pallas_call(
        last_final_kernel,
        out_shape=jax.ShapeDtypeStruct((tokens, columns), BF),
        in_specs=[vmem] * 6 + [hbm],
        out_specs=hbm,
        scratch_shapes=[
            pltpu.VMEM((WINDOW, half * HEAD_DIM), BF),
            pltpu.SemaphoreType.DMA((1,)),
        ],
        input_output_aliases={6: 0},
        compiler_params=grant,
        cost_estimate=pl.CostEstimate(flops=1 << 20, bytes_accessed=3 << 20, transcendentals=1 << 19),
        name="last",
    )(answered, lin, win_b, sum_b, top_b, gain_b, out)


def solution(mesh):
    tokens = P(("groups", "seq"), "head")
    return jax.shard_map(
        body, mesh=mesh, in_specs=(tokens,) * 5 + (P("head"),), out_specs=tokens, check_vma=False
    )
```

```python
import functools

import jax
import jax.numpy as jnp
from jax import lax
from jax.experimental import pallas as pl
from jax.experimental.pallas import tpu as pltpu
from jax.sharding import PartitionSpec as P

HEAD_DIM = 128
WINDOW = 512
TILE = 256
NEG = -(2.0**100)
SCALE = HEAD_DIM ** (-0.5) * 1.4426950408889634
BF = jnp.bfloat16
F32 = jnp.float32
GRANT = 16 << 20
LA = 4194304000
LB = 1048576000
SV = 314572800
PR = 1 << 30
RL = 104857
FN = 2097152000


def feature_rows(width):
    return -(-(width * (width + 1) // 2 + width + 1) // 16) * 16


def state_rows(heads, width):
    return heads * feature_rows(width) + 16


def answer_rows(heads):
    return -(-4 * heads * (WINDOW // TILE) // 16) * 16


def nt(a, b):
    return lax.dot_general(a, b, (((1,), (1,)), ((), ())), preferred_element_type=F32)


def nn(a, b):
    return jnp.dot(a, b, preferred_element_type=F32)


def phi_rows(x, query):
    width, tokens = x.shape
    half = width // 2
    scale = 0.5**0.5 * width ** (-0.5)
    twice = jnp.concatenate([x, x], 0)
    rows = []
    for d in range(half):
        prod = ((x * twice[d : d + width]) * scale).astype(BF)
        if query and d:
            prod = prod * 2
        rows.append(prod)
    rows.append((x * width ** (-0.25)).astype(BF))
    cross = (x[:half] * x[half:]) * scale
    if query:
        cross = cross * 2
    pad = feature_rows(width) - (half * width + width + half)
    last = lax.broadcasted_iota(jnp.int32, (pad, tokens), 0)
    const = jnp.where(last == 0, 1.0, 0.0)
    rows.append(jnp.concatenate([cross, const], 0).astype(BF))
    return jnp.concatenate(rows, 0)


def with_ones(v):
    return jnp.concatenate([v, jnp.ones_like(v)], 1)


def lanes_of(h, count=1):
    return pl.ds(pl.multiple_of(h * HEAD_DIM, HEAD_DIM), count * HEAD_DIM)


def causal_masks():
    row = lax.broadcasted_iota(jnp.int32, (TILE, TILE), 0)
    col = lax.broadcasted_iota(jnp.int32, (TILE, TILE), 1)
    return col <= row, col > row


def prepare_kernel(kf_hbm, q_hbm, k_hbm, v_hbm, kp_ref, vp_ref, qb_ref, own_ref, before_ref, kf_ref, v_ref, sems, *, heads, width):
    feats = feature_rows(width)
    base = heads * feats
    tokens = v_ref.shape[0]
    ahead = heads // 2 * HEAD_DIM
    tail = pl.ds(tokens - WINDOW, WINDOW)
    fetch = pltpu.make_async_copy(kf_hbm, kf_ref, sems.at[3])
    fetch.start()
    whole = pltpu.make_async_copy(v_hbm, v_ref, sems.at[4])
    whole.start()
    copies = [
        pltpu.make_async_copy(k_hbm.at[tail, :ahead], kp_ref, sems.at[0]),
        pltpu.make_async_copy(v_hbm.at[tail, :ahead], vp_ref, sems.at[1]),
        pltpu.make_async_copy(q_hbm.at[:WINDOW, ahead:], qb_ref, sems.at[2]),
    ]
    for copy in copies:
        copy.start()
    fetch.wait()
    phis = [phi_rows(kf_ref[h * width : (h + 1) * width, :].astype(F32), False) for h in range(heads)]
    lane = lax.broadcasted_iota(jnp.int32, (feats, HEAD_DIM), 1)
    norms = jnp.zeros((feats, HEAD_DIM), F32)
    whole.wait()
    for h in range(heads):
        total = None
        for t in range(tokens // TILE):
            at = slice(t * TILE, (t + 1) * TILE)
            s = nn(phis[h][:, at], with_ones(v_ref[at, h * HEAD_DIM : (h + 1) * HEAD_DIM]))
            total = s if t == 0 else total + s
            if t < tokens // TILE - 1:
                before_ref[t, h * feats : (h + 1) * feats, :] = total
        own_ref[h * feats : (h + 1) * feats, :] = total[:, :HEAD_DIM].astype(BF)
        norms = jnp.where(lane == h, total[:, HEAD_DIM:], norms)
    norms = jnp.concatenate([norms, jnp.zeros((2 * HEAD_DIM - feats, HEAD_DIM), F32)], 0).T[:8]
    own_ref[base:, :] = jnp.concatenate([norms[:, :HEAD_DIM], norms[:, HEAD_DIM:]], 0).astype(BF)
    for copy in copies:
        copy.wait()
    top = kp_ref[:16, :]
    row = lax.broadcasted_iota(jnp.int32, top.shape, 0)
    kp_ref[:16, :] = jnp.where(row == 0, jnp.ones((), BF), top)


def softmax_parts(jobs, ahead=2, coarse=False):
    scores = []
    for i in range(len(jobs)):
        while len(scores) < min(len(jobs), i + 1 + ahead):
            query, key = jobs[len(scores)][:2]
            scores.append(nt(query(), key()))
        _, _, value, first, last, use = jobs[i]
        s, scores[i] = scores[i], None
        parts = [s[:, at : at + TILE] for at in range(0, s.shape[1], TILE)]
        if first is not None:
            parts[0] = jnp.where(first, parts[0], NEG)
        if last is not None:
            parts[-1] = jnp.where(last, parts[-1], NEG)
        top = jnp.max(functools.reduce(jnp.maximum, parts), 1, keepdims=True)
        if coarse:
            top = top.astype(BF).astype(F32)
        p = jnp.concatenate([jnp.exp2((part - top) * SCALE).astype(BF) for part in parts], 1)
        acc = nn(p, with_ones(value()))
        use(top, acc[:, :HEAD_DIM], acc[:, HEAD_DIM:])


def local_kernel(q_ref, k_ref, v_ref, qf_ref, kf_ref, num_ref, den_ref, win_ref, sum_ref, top_ref, phi_ref, *, start_head, width):
    causal, beyond = causal_masks()
    tokens = q_ref.shape[0]
    feats = feature_rows(width)

    jobs = []

    def job(g, start):
        h = g + start_head
        at = slice(start, start + TILE)
        keys = slice(max(0, start - WINDOW), start + TILE)
        lanes = slice(g * HEAD_DIM, (g + 1) * HEAD_DIM)
        wide = slice(h * HEAD_DIM, (h + 1) * HEAD_DIM)

        def use(top, out, total):
            win_ref[at, lanes] = out
            sum_ref[at, lanes] = total
            if start < WINDOW:
                top_ref[at, lanes] = jnp.broadcast_to(top, (TILE, HEAD_DIM))
            r = nn(phi_ref[g, at, HEAD_DIM:], kfs[g][:, at])
            part = width ** (-0.25)
            t = jnp.where(causal, (r * (0.5 * part * part) + part) * r + 1.0, 0.0)
            both = nn(t.astype(BF), with_ones(v_ref[at, wide]))
            num_ref[at, lanes] = both[:, :HEAD_DIM]
            den_ref[at, lanes] = both[:, HEAD_DIM:]

        first = beyond if start >= WINDOW else None
        jobs.append((lambda: q_ref[at, wide], lambda: k_ref[keys, wide], lambda: v_ref[keys, wide], first, causal, use))

    kfs = []
    for g in range(num_ref.shape[1] // HEAD_DIM):
        h = g + start_head
        rows = slice(h * width, (h + 1) * width)
        phi_ref[g] = phi_rows(qf_ref[rows, :].astype(F32), True).astype(F32).T.astype(BF)
        kfs.append(jnp.concatenate([kf_ref[rows, :], jnp.zeros((feats - HEAD_DIM - width, tokens), BF)], 0))
        for start in range(0, tokens, TILE):
            job(g, start)
    softmax_parts(jobs)


def serve_kernel(_, qb_ref, k_ref, v_ref, __, out_ref, *, behind):
    _, beyond = causal_masks()
    base = k_ref.shape[0] - WINDOW
    count = qb_ref.shape[1] // HEAD_DIM
    lane = lax.broadcasted_iota(jnp.int32, (TILE, HEAD_DIM), 1)
    jobs = []
    stats = [jnp.zeros((TILE, HEAD_DIM), F32) for _ in range(WINDOW // TILE)]

    def job(start, g):
        at = slice(start, start + TILE)
        keys = slice(base + start, base + WINDOW)
        lanes = slice(g * HEAD_DIM, (g + 1) * HEAD_DIM)
        wide = slice((behind + g) * HEAD_DIM, (behind + g + 1) * HEAD_DIM)

        def use(top, out, total):
            out_ref[at, lanes] = out.astype(BF)
            stat = jnp.where(lane == g, top, stats[start // TILE])
            stats[start // TILE] = jnp.where(lane == count + g, total, stat)

        jobs.append((lambda: qb_ref[at, lanes], lambda: k_ref[keys, wide], lambda: v_ref[keys, wide], beyond, None, use))

    for start in range(0, WINDOW, TILE):
        for g in range(count):
            job(start, g)
    softmax_parts(jobs, coarse=True)
    rows = []
    for stat in stats:
        stat = stat.T[: 2 * count]
        top, total = stat[:count], stat[count:]
        high = total.astype(BF).astype(F32)
        middle = (total - high).astype(BF).astype(F32)
        rows += [top, high, middle, total - high - middle]
    rows.append(jnp.zeros((out_ref.shape[0] - WINDOW - 4 * count * len(stats), TILE), F32))
    rows = [part for part in rows if part.shape[0]]
    out_ref[WINDOW:, :] = jnp.concatenate(rows, 0).astype(BF)


def merged(window, mine, total, top, out, count, later):
    top = jnp.where(later, top, 2 * NEG)
    most = jnp.maximum(mine, top)
    here = jnp.exp2((mine - most) * SCALE)
    there = jnp.exp2((top - most) * SCALE)
    return window * here + out * there, total * here + count * there


def power_of(mixed):
    return jnp.mean(mixed * mixed, 1, keepdims=True) + 1e-05


def normed(mixed, power, gain):
    return (mixed * lax.rsqrt(power) * gain).astype(BF)


def halo_jobs(q_ref, kp_ref, vp_ref, win_ref, sum_ref, top_ref, near_ref, both_ref):
    _, beyond = causal_masks()
    later = kp_ref[:1, :1].astype(F32) > 0
    jobs = []

    def job(g, start):
        at = slice(start, start + TILE)
        keys = slice(start, WINDOW)
        cols = slice(g * HEAD_DIM, (g + 1) * HEAD_DIM)

        def use(top, out, total):
            near_ref[at, cols], both_ref[at, cols] = merged(
                win_ref[at, cols], top_ref[at, cols], sum_ref[at, cols], top, out, total, later
            )

        jobs.append((lambda: q_ref[at, cols], lambda: kp_ref[keys, cols], lambda: vp_ref[keys, cols], beyond, None, use))

    for g in range(kp_ref.shape[1] // HEAD_DIM):
        for start in range(0, WINDOW, TILE):
            job(g, start)
    return jobs


def first_final_kernel(q_ref, kp_ref, vp_ref, top_ref, *refs, heads, width):
    halves = [refs[:5], refs[5:10]]
    *prior_refs, before_ref, gain_hbm, out_hbm, lin_ref, gain_b_ref, gain_ref, near_ref, both_ref, out_ref, sems = refs[10:]
    count = heads // 2
    tokens = halves[0][0].shape[0]
    feats = feature_rows(width)
    base = heads * feats
    fetch = pltpu.make_async_copy(gain_hbm, gain_ref, sems.at[heads])
    fetch.start()

    def prior(rows):
        return functools.reduce(jnp.add, [ref[rows, :].astype(F32) for ref in prior_refs])

    tail = jnp.concatenate([prior(slice(base, base + 16)), jnp.zeros((HEAD_DIM - 16, HEAD_DIM), F32)], 0).T

    def state(h):
        norm = [
            jnp.broadcast_to(tail[:, h : h + 1], (HEAD_DIM, HEAD_DIM)),
            jnp.broadcast_to(tail[: feats - HEAD_DIM, 8 + h : 9 + h], (feats - HEAD_DIM, HEAD_DIM)),
        ]
        return jnp.concatenate([prior(slice(h * feats, (h + 1) * feats)), jnp.concatenate(norm, 0)], 1)

    softmax_parts(halo_jobs(q_ref, kp_ref, vp_ref, halves[0][2], halves[0][3], top_ref, near_ref, both_ref))
    order = [(h, start) for h in list(range(count, heads)) + list(range(count)) for start in range(0, tokens, TILE)]
    states, lins, copies = {}, [], []
    for i, (h, start) in enumerate(order):
        while len(lins) < min(len(order), i + 3):
            hn, sn = order[len(lins)]
            rows = slice(hn * feats, (hn + 1) * feats)
            if hn not in states:
                states[hn] = state(hn)
            both = states[hn] if sn == 0 else states[hn] + before_ref[sn // TILE - 1, rows, :]
            lins.append(nn(halves[hn // count][4][hn % count, sn : sn + TILE, :], both.astype(BF)))
        lin, lins[i] = lins[i], None
        part, g = h // count, h % count
        num_ref, den_ref, win_ref, sum_ref = halves[part][:4]
        at = slice(start, start + TILE)
        cols = slice(g * HEAD_DIM, (g + 1) * HEAD_DIM)
        wide = slice(h * HEAD_DIM, (h + 1) * HEAD_DIM)
        num = num_ref[at, cols] + lin[:, :HEAD_DIM]
        den = den_ref[at, cols] + lin[:, HEAD_DIM:]
        if start < WINDOW and part == 1:
            lin_ref[at, cols] = num / den
        else:
            if not copies and start == WINDOW:
                fetch.wait()
                gain_b_ref[...] = gain_ref[:, count * HEAD_DIM :]
            if start < WINDOW:
                window, total = near_ref[at, cols], both_ref[at, cols]
            else:
                window, total = win_ref[at, cols], sum_ref[at, cols]
            mixed = num / den + window / total
            out_ref[at, wide] = normed(mixed, power_of(mixed), gain_ref[:, wide])
        if start + TILE == tokens:
            area = (pl.ds(WINDOW * part, tokens - WINDOW * part), pl.ds(h * HEAD_DIM, HEAD_DIM))
            copies.append(pltpu.make_async_copy(out_ref.at[area], out_hbm.at[area], sems.at[h]))
            copies[-1].start()
    for copy in copies:
        copy.wait()


def last_final_kernel(ob_ref, lin_ref, win_ref, sum_ref, top_ref, gain_ref, _, out_hbm, out_ref, sems):
    count = lin_ref.shape[1] // HEAD_DIM
    ahead = out_hbm.shape[1] - count * HEAD_DIM
    stats = []
    n = 2 * count
    got = ob_ref[WINDOW:, :].astype(F32)
    for i in range(WINDOW // TILE):
        top, high, middle, low = (got[(4 * i + j) * count : (4 * i + j + 1) * count] for j in range(4))
        stats += [top, high + middle + low]
    stats.append(jnp.zeros((HEAD_DIM - count * len(stats), TILE), F32))
    stats = jnp.concatenate(stats, 0).T
    parts = [(start, g) for start in range(0, WINDOW, TILE) for g in range(count)]

    def place(start, g):
        return slice(start, start + TILE), slice(g * HEAD_DIM, (g + 1) * HEAD_DIM)

    def stat(start, lane):
        lane += start // TILE * n
        return stats[:, lane : lane + 1]

    windows = []
    for start, g in parts:
        at = place(start, g)
        total = stat(start, count + g)
        windows.append(
            merged(win_ref[at], top_ref[at], sum_ref[at], stat(start, g), ob_ref[at].astype(F32), total, total > 0)
        )
    mixed = [lin_ref[place(*part)] + window / total for part, (window, total) in zip(parts, windows)]
    powers = [power_of(m) for m in mixed]
    for part, m, power in zip(parts, mixed, powers):
        at = place(*part)
        out_ref[at] = normed(m, power, gain_ref[:, at[1]])
    copy = pltpu.make_async_copy(out_ref, out_hbm.at[:WINDOW, ahead:], sems.at[0])
    copy.start()
    copy.wait()


def relay_kernel(own_ref, got_ref, _, sum_ref, pass_ref):
    sum_ref[...] = own_ref[...] + got_ref[...]


def shifted(value, axis, steps):
    count = lax.axis_size(axis)
    pairs = [(i, i + steps) for i in range(count) if 0 <= i + steps < count]
    return lax.ppermute(value, axis, pairs)


def body(q_feat, k_feat, swa_query, swa_key, values, gain):
    tokens, columns = swa_query.shape
    heads = columns // HEAD_DIM
    half = heads // 2
    width = q_feat.shape[1] // heads
    feats = feature_rows(width)
    rows = state_rows(heads, width)
    count = lax.axis_size("seq")
    vmem = pl.BlockSpec(memory_space=pltpu.VMEM)
    hbm = pl.BlockSpec(memory_space=pltpu.HBM)
    grant = pltpu.CompilerParams(vmem_limit_bytes=GRANT)
    qft, kft = q_feat.T, k_feat.T

    in_hbm = lambda *arrays: [pltpu.with_memory_space_constraint(a, pltpu.HBM) for a in arrays]
    kp, vp, qb, own, before = pl.pallas_call(
        functools.partial(prepare_kernel, heads=heads, width=width),
        out_shape=(
            jax.ShapeDtypeStruct((WINDOW, half * HEAD_DIM), BF),
            jax.ShapeDtypeStruct((WINDOW, half * HEAD_DIM), BF),
            jax.ShapeDtypeStruct((WINDOW, half * HEAD_DIM), BF),
            jax.ShapeDtypeStruct((rows, HEAD_DIM), BF),
            jax.ShapeDtypeStruct((tokens // TILE - 1, heads * feats, 2 * HEAD_DIM), F32),
        ),
        in_specs=[hbm] * 4,
        out_specs=(vmem,) * 5,
        scratch_shapes=[
            pltpu.VMEM(kft.shape, BF),
            pltpu.VMEM((tokens, columns), BF),
            pltpu.SemaphoreType.DMA((5,)),
        ],
        compiler_params=grant,
        cost_estimate=pl.CostEstimate(flops=1 << 30, bytes_accessed=3 << 20, transcendentals=0),
        name="prepare",
    )(*in_hbm(kft, swa_query, swa_key, values))

    def local(start_head, flops):
        wide = jax.ShapeDtypeStruct((tokens, half * HEAD_DIM), F32)
        near = jax.ShapeDtypeStruct((WINDOW, half * HEAD_DIM), F32)
        return pl.pallas_call(
            functools.partial(local_kernel, start_head=start_head, width=width),
            out_shape=(wide, wide, wide, wide, near, jax.ShapeDtypeStruct((half, tokens, feats), BF)),
            in_specs=[vmem] * 5,
            out_specs=(vmem,) * 6,
            compiler_params=grant,
            cost_estimate=pl.CostEstimate(flops=flops, bytes_accessed=1 << 20, transcendentals=1 << 10),
            name="local",
        )(swa_query, swa_key, values, qft, kft)

    local_a = local(0, LA)

    def serve(asked):
        return pl.pallas_call(
            functools.partial(serve_kernel, behind=half),
            out_shape=jax.ShapeDtypeStruct((WINDOW + answer_rows(half), half * HEAD_DIM), BF),
            in_specs=[vmem] * 5,
            out_specs=vmem,
            compiler_params=grant,
            cost_estimate=pl.CostEstimate(flops=SV, bytes_accessed=1 << 20, transcendentals=1 << 10),
            name="serve",
        )(halo[0], asked, swa_key, values, local_a[4])

    def relay(got, passed):
        return pl.pallas_call(
            relay_kernel,
            out_shape=(jax.ShapeDtypeStruct(own.shape, BF), jax.ShapeDtypeStruct(passed.shape, BF)),
            in_specs=[vmem] * 3,
            out_specs=(vmem,) * 2,
            input_output_aliases={2: 1},
            compiler_params=grant,
            cost_estimate=pl.CostEstimate(flops=RL, bytes_accessed=1 << 19, transcendentals=0),
            name="relay",
        )(own, got, passed)

    if count <= 4:
        running, prior = own, []
        for i in range(count - 1):
            got = lax.ppermute(running, "seq", [(i, i + 1)])
            prior.append(got)
            if i == 0:
                halo_key = shifted(kp, "seq", 1)
                asked = shifted(qb, "seq", -1)
                running, vp = relay(got, vp)
                halo = halo_key, shifted(vp, "seq", 1)
                answer = serve(asked)
            elif i == 1:
                running, answer = relay(got, answer)
            else:
                running = own + got
    else:
        running, prior, distance = own, [], 1
        halo = shifted(kp, "seq", 1), shifted(vp, "seq", 1)
        answer = serve(shifted(qb, "seq", -1))
        while distance < count:
            got = shifted(running, "seq", distance)
            prior.append(got)
            running = running + got
            distance *= 2

    answered = shifted(answer, "seq", 1)
    local_b = local(half, LB)

    num_a, den_a, win_a, sum_a, top_a, phi_a = local_a
    num_b, den_b, win_b, sum_b, top_b, phi_b = local_b
    gain_row = in_hbm(gain.reshape(1, columns))
    near = jax.ShapeDtypeStruct((WINDOW, half * HEAD_DIM), F32)
    operands = (swa_query, *halo, top_a, num_a, den_a, win_a, sum_a, phi_a, num_b, den_b, win_b, sum_b, phi_b, *prior, before)
    out, lin, gain_b = pl.pallas_call(
        functools.partial(first_final_kernel, heads=heads, width=width),
        out_shape=(
            jax.ShapeDtypeStruct((tokens, columns), BF),
            near,
            jax.ShapeDtypeStruct((1, half * HEAD_DIM), F32),
        ),
        in_specs=[vmem] * len(operands) + [hbm],
        out_specs=(hbm, vmem, vmem),
        scratch_shapes=[
            pltpu.VMEM((1, columns), F32),
            pltpu.VMEM(near.shape, F32),
            pltpu.VMEM(near.shape, F32),
            pltpu.VMEM((tokens, columns), BF),
            pltpu.SemaphoreType.DMA((heads + 1,)),
        ],
        compiler_params=grant,
        cost_estimate=pl.CostEstimate(flops=FN, bytes_accessed=12 << 20, transcendentals=1 << 20),
        name="final",
    )(*operands, *gain_row)
    return pl.pallas_call(
        last_final_kernel,
        out_shape=jax.ShapeDtypeStruct((tokens, columns), BF),
        in_specs=[vmem] * 6 + [hbm],
        out_specs=hbm,
        scratch_shapes=[
            pltpu.VMEM((WINDOW, half * HEAD_DIM), BF),
            pltpu.SemaphoreType.DMA((1,)),
        ],
        input_output_aliases={6: 0},
        compiler_params=grant,
        cost_estimate=pl.CostEstimate(flops=1 << 20, bytes_accessed=3 << 20, transcendentals=1 << 19),
        name="last",
    )(answered, lin, win_b, sum_b, top_b, gain_b, out)


def solution(mesh):
    tokens = P(("groups", "seq"), "head")
    return jax.shard_map(
        body, mesh=mesh, in_specs=(tokens,) * 5 + (P("head"),), out_specs=tokens, check_vma=False
    )
```

```python
import functools

import jax
import jax.numpy as jnp
from jax import lax
from jax.experimental import pallas as pl
from jax.experimental.pallas import tpu as pltpu
from jax.sharding import PartitionSpec as P

HEAD_DIM = 128
WINDOW = 512
TILE = 256
NEG = -(2.0**100)
SCALE = HEAD_DIM ** (-0.5) * 1.4426950408889634
BF = jnp.bfloat16
F32 = jnp.float32
GRANT = 16 << 20
LA = 4194304000
LB = 1048576000
SV = 314572800
PR = 1 << 30
RL = 104857
FN = 2097152000


def feature_rows(width):
    return -(-(width * (width + 1) // 2 + width + 1) // 16) * 16


def state_rows(heads, width):
    return heads * feature_rows(width)


def answer_rows(heads):
    return -(-4 * heads * (WINDOW // TILE) // 16) * 16


def nt(a, b):
    return lax.dot_general(a, b, (((1,), (1,)), ((), ())), preferred_element_type=F32)


def nn(a, b):
    return jnp.dot(a, b, preferred_element_type=F32)


def phi_rows(x, query):
    width, tokens = x.shape
    half = width // 2
    scale = 0.5**0.5 * width ** (-0.5)
    twice = jnp.concatenate([x, x], 0)
    rows = []
    for d in range(half):
        prod = ((x * twice[d : d + width]) * scale).astype(BF)
        if query and d:
            prod = prod * 2
        rows.append(prod)
    rows.append((x * width ** (-0.25)).astype(BF))
    cross = (x[:half] * x[half:]) * scale
    if query:
        cross = cross * 2
    pad = feature_rows(width) - (half * width + width + half)
    last = lax.broadcasted_iota(jnp.int32, (pad, tokens), 0)
    const = jnp.where(last == 0, 1.0, 0.0)
    rows.append(jnp.concatenate([cross, const], 0).astype(BF))
    return jnp.concatenate(rows, 0)


def with_ones(v):
    return jnp.concatenate([v, jnp.ones_like(v)], 1)


def lanes_of(h, count=1):
    return pl.ds(pl.multiple_of(h * HEAD_DIM, HEAD_DIM), count * HEAD_DIM)


def causal_masks():
    row = lax.broadcasted_iota(jnp.int32, (TILE, TILE), 0)
    col = lax.broadcasted_iota(jnp.int32, (TILE, TILE), 1)
    return col <= row, col > row


def prepare_kernel(kf_hbm, q_hbm, k_hbm, v_hbm, kp_ref, vp_ref, qb_ref, own_ref, before_ref, kf_ref, v_ref, sems, *, heads, width):
    feats = feature_rows(width)
    tokens = v_ref.shape[0]
    ahead = heads // 2 * HEAD_DIM
    tail = pl.ds(tokens - WINDOW, WINDOW)
    fetch = pltpu.make_async_copy(kf_hbm, kf_ref, sems.at[3])
    fetch.start()
    whole = pltpu.make_async_copy(v_hbm, v_ref, sems.at[4])
    whole.start()
    copies = [
        pltpu.make_async_copy(k_hbm.at[tail, :ahead], kp_ref, sems.at[0]),
        pltpu.make_async_copy(v_hbm.at[tail, :ahead], vp_ref, sems.at[1]),
        pltpu.make_async_copy(q_hbm.at[:WINDOW, ahead:], qb_ref, sems.at[2]),
    ]
    for copy in copies:
        copy.start()
    fetch.wait()
    phis = [phi_rows(kf_ref[h * width : (h + 1) * width, :].astype(F32), False) for h in range(heads)]
    lane = lax.broadcasted_iota(jnp.int32, (feats, HEAD_DIM), 1)
    norms = jnp.zeros((feats, HEAD_DIM), F32)
    whole.wait()
    for h in range(heads):
        total = None
        for t in range(tokens // TILE):
            at = slice(t * TILE, (t + 1) * TILE)
            s = nn(phis[h][:, at], with_ones(v_ref[at, h * HEAD_DIM : (h + 1) * HEAD_DIM]))
            total = s if t == 0 else total + s
            if t < tokens // TILE - 1:
                before_ref[t, h * feats : (h + 1) * feats, :] = total
        own_ref[h * feats : (h + 1) * feats, :] = total[:, :HEAD_DIM].astype(BF)
        norms = jnp.where(lane == h, total[:, HEAD_DIM:], norms)
    norms = jnp.concatenate([norms, jnp.zeros((2 * HEAD_DIM - feats, HEAD_DIM), F32)], 0).T[:8]
    for h in range(heads):
        spare = (h + 1) * feats - 2
        own_ref[spare : spare + 1, :] = norms[h : h + 1, :HEAD_DIM].astype(BF)
        own_ref[spare + 1 : spare + 2, :] = norms[h : h + 1, HEAD_DIM:].astype(BF)
    for copy in copies:
        copy.wait()
    top = kp_ref[:16, :]
    row = lax.broadcasted_iota(jnp.int32, top.shape, 0)
    kp_ref[:16, :] = jnp.where(row == 0, jnp.ones((), BF), top)


def softmax_parts(jobs, ahead=2, coarse=False):
    scores = []
    for i in range(len(jobs)):
        while len(scores) < min(len(jobs), i + 1 + ahead):
            query, key = jobs[len(scores)][:2]
            scores.append(nt(query(), key()))
        _, _, value, first, last, use = jobs[i]
        s, scores[i] = scores[i], None
        parts = [s[:, at : at + TILE] for at in range(0, s.shape[1], TILE)]
        if first is not None:
            parts[0] = jnp.where(first, parts[0], NEG)
        if last is not None:
            parts[-1] = jnp.where(last, parts[-1], NEG)
        top = jnp.max(functools.reduce(jnp.maximum, parts), 1, keepdims=True)
        if coarse:
            top = top.astype(BF).astype(F32)
        p = jnp.concatenate([jnp.exp2((part - top) * SCALE).astype(BF) for part in parts], 1)
        acc = nn(p, with_ones(value()))
        use(top, acc[:, :HEAD_DIM], acc[:, HEAD_DIM:])


def local_kernel(q_ref, k_ref, v_ref, qf_ref, kf_ref, num_ref, den_ref, win_ref, sum_ref, top_ref, phi_ref, *, start_head, width):
    causal, beyond = causal_masks()
    tokens = q_ref.shape[0]
    feats = feature_rows(width)

    jobs = []

    def job(g, start):
        h = g + start_head
        at = slice(start, start + TILE)
        keys = slice(max(0, start - WINDOW), start + TILE)
        lanes = slice(g * HEAD_DIM, (g + 1) * HEAD_DIM)
        wide = slice(h * HEAD_DIM, (h + 1) * HEAD_DIM)

        def use(top, out, total):
            win_ref[at, lanes] = out
            sum_ref[at, lanes] = total
            if start < WINDOW:
                top_ref[at, lanes] = jnp.broadcast_to(top, (TILE, HEAD_DIM))
            r = nn(phi_ref[g, at, HEAD_DIM:], kfs[g][:, at])
            part = width ** (-0.25)
            t = jnp.where(causal, (r * (0.5 * part * part) + part) * r + 1.0, 0.0)
            both = nn(t.astype(BF), with_ones(v_ref[at, wide]))
            num_ref[at, lanes] = both[:, :HEAD_DIM]
            den_ref[at, lanes] = both[:, HEAD_DIM:]

        first = beyond if start >= WINDOW else None
        jobs.append((lambda: q_ref[at, wide], lambda: k_ref[keys, wide], lambda: v_ref[keys, wide], first, causal, use))

    kfs = []
    for g in range(num_ref.shape[1] // HEAD_DIM):
        h = g + start_head
        rows = slice(h * width, (h + 1) * width)
        phi_ref[g] = phi_rows(qf_ref[rows, :].astype(F32), True).astype(F32).T.astype(BF)
        kfs.append(jnp.concatenate([kf_ref[rows, :], jnp.zeros((feats - HEAD_DIM - width, tokens), BF)], 0))
        for start in range(0, tokens, TILE):
            job(g, start)
    softmax_parts(jobs)


def serve_kernel(_, qb_ref, k_ref, v_ref, __, out_ref, *, behind):
    _, beyond = causal_masks()
    base = k_ref.shape[0] - WINDOW
    count = qb_ref.shape[1] // HEAD_DIM
    lane = lax.broadcasted_iota(jnp.int32, (TILE, HEAD_DIM), 1)
    jobs = []
    stats = [jnp.zeros((TILE, HEAD_DIM), F32) for _ in range(WINDOW // TILE)]

    def job(start, g):
        at = slice(start, start + TILE)
        keys = slice(base + start, base + WINDOW)
        lanes = slice(g * HEAD_DIM, (g + 1) * HEAD_DIM)
        wide = slice((behind + g) * HEAD_DIM, (behind + g + 1) * HEAD_DIM)

        def use(top, out, total):
            out_ref[at, lanes] = out.astype(BF)
            stat = jnp.where(lane == g, top, stats[start // TILE])
            stats[start // TILE] = jnp.where(lane == count + g, total, stat)

        jobs.append((lambda: qb_ref[at, lanes], lambda: k_ref[keys, wide], lambda: v_ref[keys, wide], beyond, None, use))

    for start in range(0, WINDOW, TILE):
        for g in range(count):
            job(start, g)
    softmax_parts(jobs, coarse=True)
    rows = []
    for stat in stats:
        stat = stat.T[: 2 * count]
        top, total = stat[:count], stat[count:]
        high = total.astype(BF).astype(F32)
        middle = (total - high).astype(BF).astype(F32)
        rows += [top, high, middle, total - high - middle]
    rows.append(jnp.zeros((out_ref.shape[0] - WINDOW - 4 * count * len(stats), TILE), F32))
    rows = [part for part in rows if part.shape[0]]
    out_ref[WINDOW:, :] = jnp.concatenate(rows, 0).astype(BF)


def merged(window, mine, total, top, out, count, later):
    top = jnp.where(later, top, 2 * NEG)
    most = jnp.maximum(mine, top)
    here = jnp.exp2((mine - most) * SCALE)
    there = jnp.exp2((top - most) * SCALE)
    return window * here + out * there, total * here + count * there


def power_of(mixed):
    return jnp.mean(mixed * mixed, 1, keepdims=True) + 1e-05


def normed(mixed, power, gain):
    return (mixed * lax.rsqrt(power) * gain).astype(BF)


def halo_jobs(q_ref, kp_ref, vp_ref, win_ref, sum_ref, top_ref, near_ref, both_ref):
    _, beyond = causal_masks()
    later = kp_ref[:1, :1].astype(F32) > 0
    jobs = []

    def job(g, start):
        at = slice(start, start + TILE)
        keys = slice(start, WINDOW)
        cols = slice(g * HEAD_DIM, (g + 1) * HEAD_DIM)

        def use(top, out, total):
            near_ref[at, cols], both_ref[at, cols] = merged(
                win_ref[at, cols], top_ref[at, cols], sum_ref[at, cols], top, out, total, later
            )

        jobs.append((lambda: q_ref[at, cols], lambda: kp_ref[keys, cols], lambda: vp_ref[keys, cols], beyond, None, use))

    for g in range(kp_ref.shape[1] // HEAD_DIM):
        for start in range(0, WINDOW, TILE):
            job(g, start)
    return jobs


def first_final_kernel(q_ref, kp_ref, vp_ref, top_ref, *refs, heads, width):
    halves = [refs[:5], refs[5:10]]
    *prior_refs, before_ref, gain_hbm, out_hbm, lin_ref, gain_b_ref, gain_ref, near_ref, both_ref, out_ref, sems = refs[10:]
    count = heads // 2
    tokens = halves[0][0].shape[0]
    feats = feature_rows(width)
    fetch = pltpu.make_async_copy(gain_hbm, gain_ref, sems.at[heads])
    fetch.start()

    def prior(rows):
        return functools.reduce(jnp.add, [ref[rows, :].astype(F32) for ref in prior_refs])

    tail = [prior(slice((h + 1) * feats - 16, (h + 1) * feats)) for h in range(heads)]
    tail = jnp.concatenate(tail + [jnp.zeros((HEAD_DIM - 16 * heads, HEAD_DIM), F32)], 0).T

    def state(h):
        norm = [
            jnp.broadcast_to(tail[:, 16 * h + 14 : 16 * h + 15], (HEAD_DIM, HEAD_DIM)),
            jnp.broadcast_to(tail[: feats - HEAD_DIM, 16 * h + 15 : 16 * h + 16], (feats - HEAD_DIM, HEAD_DIM)),
        ]
        return jnp.concatenate([prior(slice(h * feats, (h + 1) * feats)), jnp.concatenate(norm, 0)], 1)

    softmax_parts(halo_jobs(q_ref, kp_ref, vp_ref, halves[0][2], halves[0][3], top_ref, near_ref, both_ref))
    order = [(h, start) for h in list(range(count, heads)) + list(range(count)) for start in range(0, tokens, TILE)]
    states, lins, copies = {}, [], []
    for i, (h, start) in enumerate(order):
        while len(lins) < min(len(order), i + 3):
            hn, sn = order[len(lins)]
            rows = slice(hn * feats, (hn + 1) * feats)
            if hn not in states:
                states[hn] = state(hn)
            both = states[hn] if sn == 0 else states[hn] + before_ref[sn // TILE - 1, rows, :]
            lins.append(nn(halves[hn // count][4][hn % count, sn : sn + TILE, :], both.astype(BF)))
        lin, lins[i] = lins[i], None
        part, g = h // count, h % count
        num_ref, den_ref, win_ref, sum_ref = halves[part][:4]
        at = slice(start, start + TILE)
        cols = slice(g * HEAD_DIM, (g + 1) * HEAD_DIM)
        wide = slice(h * HEAD_DIM, (h + 1) * HEAD_DIM)
        num = num_ref[at, cols] + lin[:, :HEAD_DIM]
        den = den_ref[at, cols] + lin[:, HEAD_DIM:]
        if start < WINDOW and part == 1:
            lin_ref[at, cols] = num / den
        else:
            if not copies and start == WINDOW:
                fetch.wait()
                gain_b_ref[...] = gain_ref[:, count * HEAD_DIM :]
            if start < WINDOW:
                window, total = near_ref[at, cols], both_ref[at, cols]
            else:
                window, total = win_ref[at, cols], sum_ref[at, cols]
            mixed = num / den + window / total
            out_ref[at, wide] = normed(mixed, power_of(mixed), gain_ref[:, wide])
        if start + TILE == tokens:
            area = (pl.ds(WINDOW * part, tokens - WINDOW * part), pl.ds(h * HEAD_DIM, HEAD_DIM))
            copies.append(pltpu.make_async_copy(out_ref.at[area], out_hbm.at[area], sems.at[h]))
            copies[-1].start()
    for copy in copies:
        copy.wait()


def last_final_kernel(ob_ref, lin_ref, win_ref, sum_ref, top_ref, gain_ref, _, out_hbm, out_ref, sems):
    count = lin_ref.shape[1] // HEAD_DIM
    ahead = out_hbm.shape[1] - count * HEAD_DIM
    stats = []
    n = 2 * count
    got = ob_ref[WINDOW:, :].astype(F32)
    for i in range(WINDOW // TILE):
        top, high, middle, low = (got[(4 * i + j) * count : (4 * i + j + 1) * count] for j in range(4))
        stats += [top, high + middle + low]
    stats.append(jnp.zeros((HEAD_DIM - count * len(stats), TILE), F32))
    stats = jnp.concatenate(stats, 0).T
    parts = [(start, g) for start in range(0, WINDOW, TILE) for g in range(count)]

    def place(start, g):
        return slice(start, start + TILE), slice(g * HEAD_DIM, (g + 1) * HEAD_DIM)

    def stat(start, lane):
        lane += start // TILE * n
        return stats[:, lane : lane + 1]

    windows = []
    for start, g in parts:
        at = place(start, g)
        total = stat(start, count + g)
        windows.append(
            merged(win_ref[at], top_ref[at], sum_ref[at], stat(start, g), ob_ref[at].astype(F32), total, total > 0)
        )
    mixed = [lin_ref[place(*part)] + window / total for part, (window, total) in zip(parts, windows)]
    powers = [power_of(m) for m in mixed]
    for part, m, power in zip(parts, mixed, powers):
        at = place(*part)
        out_ref[at] = normed(m, power, gain_ref[:, at[1]])
    copy = pltpu.make_async_copy(out_ref, out_hbm.at[:WINDOW, ahead:], sems.at[0])
    copy.start()
    copy.wait()


def relay_kernel(own_ref, got_ref, _, sum_ref, pass_ref):
    sum_ref[...] = own_ref[...] + got_ref[...]


def shifted(value, axis, steps):
    count = lax.axis_size(axis)
    pairs = [(i, i + steps) for i in range(count) if 0 <= i + steps < count]
    return lax.ppermute(value, axis, pairs)


def body(q_feat, k_feat, swa_query, swa_key, values, gain):
    tokens, columns = swa_query.shape
    heads = columns // HEAD_DIM
    half = heads // 2
    width = q_feat.shape[1] // heads
    feats = feature_rows(width)
    rows = state_rows(heads, width)
    count = lax.axis_size("seq")
    vmem = pl.BlockSpec(memory_space=pltpu.VMEM)
    hbm = pl.BlockSpec(memory_space=pltpu.HBM)
    grant = pltpu.CompilerParams(vmem_limit_bytes=GRANT)
    qft, kft = q_feat.T, k_feat.T

    in_hbm = lambda *arrays: [pltpu.with_memory_space_constraint(a, pltpu.HBM) for a in arrays]
    kp, vp, qb, own, before = pl.pallas_call(
        functools.partial(prepare_kernel, heads=heads, width=width),
        out_shape=(
            jax.ShapeDtypeStruct((WINDOW, half * HEAD_DIM), BF),
            jax.ShapeDtypeStruct((WINDOW, half * HEAD_DIM), BF),
            jax.ShapeDtypeStruct((WINDOW, half * HEAD_DIM), BF),
            jax.ShapeDtypeStruct((rows, HEAD_DIM), BF),
            jax.ShapeDtypeStruct((tokens // TILE - 1, heads * feats, 2 * HEAD_DIM), F32),
        ),
        in_specs=[hbm] * 4,
        out_specs=(vmem,) * 5,
        scratch_shapes=[
            pltpu.VMEM(kft.shape, BF),
            pltpu.VMEM((tokens, columns), BF),
            pltpu.SemaphoreType.DMA((5,)),
        ],
        compiler_params=grant,
        cost_estimate=pl.CostEstimate(flops=1 << 30, bytes_accessed=3 << 20, transcendentals=0),
        name="prepare",
    )(*in_hbm(kft, swa_query, swa_key, values))

    def local(start_head, flops):
        wide = jax.ShapeDtypeStruct((tokens, half * HEAD_DIM), F32)
        near = jax.ShapeDtypeStruct((WINDOW, half * HEAD_DIM), F32)
        return pl.pallas_call(
            functools.partial(local_kernel, start_head=start_head, width=width),
            out_shape=(wide, wide, wide, wide, near, jax.ShapeDtypeStruct((half, tokens, feats), BF)),
            in_specs=[vmem] * 5,
            out_specs=(vmem,) * 6,
            compiler_params=grant,
            cost_estimate=pl.CostEstimate(flops=flops, bytes_accessed=1 << 20, transcendentals=1 << 10),
            name="local",
        )(swa_query, swa_key, values, qft, kft)

    local_a = local(0, LA)

    def serve(asked):
        return pl.pallas_call(
            functools.partial(serve_kernel, behind=half),
            out_shape=jax.ShapeDtypeStruct((WINDOW + answer_rows(half), half * HEAD_DIM), BF),
            in_specs=[vmem] * 5,
            out_specs=vmem,
            compiler_params=grant,
            cost_estimate=pl.CostEstimate(flops=SV, bytes_accessed=1 << 20, transcendentals=1 << 10),
            name="serve",
        )(halo[0], asked, swa_key, values, local_a[4])

    def relay(got, passed):
        return pl.pallas_call(
            relay_kernel,
            out_shape=(jax.ShapeDtypeStruct(own.shape, BF), jax.ShapeDtypeStruct(passed.shape, BF)),
            in_specs=[vmem] * 3,
            out_specs=(vmem,) * 2,
            input_output_aliases={2: 1},
            compiler_params=grant,
            cost_estimate=pl.CostEstimate(flops=RL, bytes_accessed=1 << 19, transcendentals=0),
            name="relay",
        )(own, got, passed)

    if count <= 4:
        running, prior = own, []
        for i in range(count - 1):
            got = lax.ppermute(running, "seq", [(i, i + 1)])
            prior.append(got)
            if i == 0:
                halo_key = shifted(kp, "seq", 1)
                asked = shifted(qb, "seq", -1)
                running, vp = relay(got, vp)
                halo = halo_key, shifted(vp, "seq", 1)
                answer = serve(asked)
            elif i == 1:
                running, answer = relay(got, answer)
            else:
                running = own + got
    else:
        running, prior, distance = own, [], 1
        halo = shifted(kp, "seq", 1), shifted(vp, "seq", 1)
        answer = serve(shifted(qb, "seq", -1))
        while distance < count:
            got = shifted(running, "seq", distance)
            prior.append(got)
            running = running + got
            distance *= 2

    answered = shifted(answer, "seq", 1)
    local_b = local(half, LB)

    num_a, den_a, win_a, sum_a, top_a, phi_a = local_a
    num_b, den_b, win_b, sum_b, top_b, phi_b = local_b
    gain_row = in_hbm(gain.reshape(1, columns))
    near = jax.ShapeDtypeStruct((WINDOW, half * HEAD_DIM), F32)
    operands = (swa_query, *halo, top_a, num_a, den_a, win_a, sum_a, phi_a, num_b, den_b, win_b, sum_b, phi_b, *prior, before)
    out, lin, gain_b = pl.pallas_call(
        functools.partial(first_final_kernel, heads=heads, width=width),
        out_shape=(
            jax.ShapeDtypeStruct((tokens, columns), BF),
            near,
            jax.ShapeDtypeStruct((1, half * HEAD_DIM), F32),
        ),
        in_specs=[vmem] * len(operands) + [hbm],
        out_specs=(hbm, vmem, vmem),
        scratch_shapes=[
            pltpu.VMEM((1, columns), F32),
            pltpu.VMEM(near.shape, F32),
            pltpu.VMEM(near.shape, F32),
            pltpu.VMEM((tokens, columns), BF),
            pltpu.SemaphoreType.DMA((heads + 1,)),
        ],
        compiler_params=grant,
        cost_estimate=pl.CostEstimate(flops=FN, bytes_accessed=12 << 20, transcendentals=1 << 20),
        name="final",
    )(*operands, *gain_row)
    return pl.pallas_call(
        last_final_kernel,
        out_shape=jax.ShapeDtypeStruct((tokens, columns), BF),
        in_specs=[vmem] * 6 + [hbm],
        out_specs=hbm,
        scratch_shapes=[
            pltpu.VMEM((WINDOW, half * HEAD_DIM), BF),
            pltpu.SemaphoreType.DMA((1,)),
        ],
        input_output_aliases={6: 0},
        compiler_params=grant,
        cost_estimate=pl.CostEstimate(flops=1 << 20, bytes_accessed=3 << 20, transcendentals=1 << 19),
        name="last",
    )(answered, lin, win_b, sum_b, top_b, gain_b, out)


def solution(mesh):
    tokens = P(("groups", "seq"), "head")
    return jax.shard_map(
        body, mesh=mesh, in_specs=(tokens,) * 5 + (P("head"),), out_specs=tokens, check_vma=False
    )
```
